32 devices in a mesh: group: 2 (over y), patch: 4 (over z), head: 2 (over x), cfg: 2 (over core).
Axes of the slice: x: 2, y: 2, z: 4, core: 2. Of those that a mesh axis runs over, the one named last changes fastest.
Arguments:
- fresh_query: bfloat16 [4, 256, 2560], P(('group', 'cfg'), ('patch', 'head')), parts along dimension 0, may hold values from -32 to 32
- fresh_key: bfloat16 [4, 256, 2560], P(('group', 'cfg'), ('patch', 'head')), parts along dimension 0, may hold values from -9 to 9
- fresh_value: bfloat16 [4, 256, 2560], P(('group', 'cfg'), ('patch', 'head')), parts along dimension 0, may hold values from -12 to 12
- stale_key: bfloat16 [4, 256, 2560], P(('group', 'cfg'), 'patch', 'head'), parts along dimension 0, may hold values from -8 to 8
- stale_value: bfloat16 [4, 256, 2560], P(('group', 'cfg'), 'patch', 'head'), parts along dimension 0, may hold values from -12 to 12
- cross_query: bfloat16 [4, 256, 2560], P(('group', 'cfg'), ('patch', 'head')), parts along dimension 0, may hold values from -32 to 32
- text_key: bfloat16 [4, 512, 2560], P(('group', 'cfg'), None, 'head'), parts along dimension 0, may hold values from -8 to 8
- text_value: bfloat16 [4, 512, 2560], P(('group', 'cfg'), None, 'head'), parts along dimension 0, may hold values from -12 to 12
- text_mask: int32 [4, 512], P(('group', 'cfg')), parts along dimension 0, may hold values from 0 to 1, as said below
Outputs:
- self_mixed: bfloat16 [4, 256, 2560], P(('group', 'cfg'), ('patch', 'head')), parts along dimension 0
- cross_mixed: bfloat16 [4, 256, 2560], P(('group', 'cfg'), ('patch', 'head')), parts along dimension 0
The draws below stay inside these ranges and needn't reach their ends.
There are 2 independent parts, one for each index of `group`. The reference program is written for one: setup_inputs(seed, part) draws one part's arguments, and reference() takes and returns one part's arrays. A program takes and returns all parts, laid end to end along the dimension named above; each array names one. Nothing has to cross between parts.
Inputs may be any that keep to these rules, and one draw needn't show every extreme that they name: In each branch the ones of text_mask form a prefix of 32 or more positions; in one of the two branches all 512 are ones, in the other some are zeros.
All inputs are finite; a program needn't handle non-finite values.
Results may differ from the reference program's by a relative error of at most 0.005.
Values may be sent and summed in bfloat16 or wider, within the bound.
A program may use at most 128 MiB of HBM per device.

```python
import math
import jax
import jax.numpy as jnp
from jax import lax

HEADS = 20
HD = 128
TXT = 512
HW = 2560
PATCH_TOK = 64
TOKENS = 256
N_PATCH = 4


def keys_table(key, row_count):
    columns = HEADS * HD
    return 1.5 * jax.random.truncated_normal(key, -4.0, 4.0, (2, row_count, columns), jnp.float32)


def query_table(key, row_count):
    columns = HEADS * HD
    return 1.5 * jax.random.truncated_normal(key, -4.0, 4.0, (2, row_count, columns), jnp.float32)


def draw_stale_key(key, part):
    return keys_table(jax.random.fold_in(key, 11), TOKENS).astype(jnp.bfloat16)


def draw_text_key(key, part):
    return keys_table(jax.random.fold_in(key, 13), TXT).astype(jnp.bfloat16)


def draw_fresh_query(key, part):
    return query_table(jax.random.fold_in(key, 17), TOKENS).astype(jnp.bfloat16)


def draw_cross_query(key, part):
    return query_table(jax.random.fold_in(key, 19), TOKENS).astype(jnp.bfloat16)


def draw_text_mask(key, part):
    lowest = max(2, TXT // 16)
    partial_length = jax.random.randint(jax.random.fold_in(key, 31), (), lowest, TXT)
    full_branch = jax.random.randint(jax.random.fold_in(key, 37), (), 0, 2)
    lengths = jnp.where(jnp.arange(2) == full_branch, TXT, partial_length)
    return (jnp.arange(TXT)[None, :] < lengths[:, None]).astype(jnp.int32)


def steps_of(stream_key, dims, split, smallest, top_value):
    factor_of = 1.0
    for dim, shards_of in split:
        draws = jax.random.uniform(jax.random.fold_in(jax.random.fold_in(stream_key, 6), dim), (shards_of,), jnp.float32, smallest / len(split), top_value / len(split))
        factor_of = factor_of * jnp.repeat(jnp.exp(draws), dims[dim] // shards_of).reshape((-1,) + (1,) * (len(dims) - 1 - dim))
    return factor_of


def bell_draw(stream_key, dims, deviation, limit, split=(), kind=jnp.bfloat16):
    array = jax.random.normal(stream_key, dims, jnp.float32) * deviation
    if len(split) > 0:
        array = steps_of(stream_key, dims, split, -0.22, 0.18) * array
    return jnp.clip(array, min=-limit, max=limit).astype(kind)


def setup_inputs(seed: int = 0, part: int = 0) -> dict:
    keys = jax.random.split(jax.random.key(seed), 10)
    part_keys = jax.random.split(jax.random.fold_in(keys[9], part), 10)
    return {
        "fresh_query": draw_fresh_query(jax.random.fold_in(jax.random.fold_in(keys[9], part), 71), part),
        "fresh_key": bell_draw(part_keys[1], (2, TOKENS, HW), 1.5, 9.0, ((0, 2), (1, 8))),
        "fresh_value": bell_draw(part_keys[2], (2, TOKENS, HW), 2.0, 12.0, ((0, 2), (1, 8))),
        "stale_key": draw_stale_key(jax.random.fold_in(jax.random.fold_in(keys[9], part), 71), part),
        "stale_value": bell_draw(part_keys[4], (2, TOKENS, HW), 2.0, 12.0, ((0, 2), (1, 4), (2, 2))),
        "cross_query": draw_cross_query(jax.random.fold_in(jax.random.fold_in(keys[9], part), 71), part),
        "text_key": draw_text_key(jax.random.fold_in(jax.random.fold_in(keys[9], part), 71), part),
        "text_value": bell_draw(part_keys[7], (2, TXT, HW), 2.0, 12.0, ((0, 2), (2, 2))),
        "text_mask": draw_text_mask(jax.random.fold_in(jax.random.fold_in(keys[9], part), 71), part),
    }


def softmax_mix(queries, all_keys, all_values, usable):
    head_queries = queries.reshape(queries.shape[0], HEADS, HD).astype(jnp.float32)
    head_keys = all_keys.reshape(all_keys.shape[0], HEADS, HD).astype(jnp.float32)
    head_values = all_values.reshape(all_values.shape[0], HEADS, HD).astype(jnp.float32)
    scores = jnp.einsum('qhd,khd->qhk', head_queries, head_keys) * (1.0 / math.sqrt(HD))
    if usable is None:
        row_top = lax.optimization_barrier(jnp.max(scores, axis=-1, keepdims=True))
        weights = jnp.exp(scores - row_top)
    else:
        row_top = lax.optimization_barrier(jnp.max(jnp.where(usable, scores, -jnp.inf), axis=-1, keepdims=True))
        weights = jnp.where(usable, jnp.exp(jnp.where(usable, scores, row_top) - row_top), 0.0)
    totals = lax.optimization_barrier(jnp.sum(weights, axis=-1, keepdims=True))
    rounded = lax.optimization_barrier(weights.astype(jnp.bfloat16)).astype(jnp.float32)
    mixture = jnp.einsum('qhk,khd->qhd', rounded, head_values) / totals
    return mixture.reshape(queries.shape[0], HEADS * HD).astype(jnp.bfloat16)

def self_branch(queries, keys_new, values_new, keys_old, values_old):

    def one_patch(patch_index):
        offset = patch_index * PATCH_TOK
        all_keys = lax.dynamic_update_slice(keys_old, lax.dynamic_slice_in_dim(keys_new, offset, PATCH_TOK, 0), (offset, jnp.int32(0)))
        all_values = lax.dynamic_update_slice(values_old, lax.dynamic_slice_in_dim(values_new, offset, PATCH_TOK, 0), (offset, jnp.int32(0)))
        return softmax_mix(lax.dynamic_slice_in_dim(queries, offset, PATCH_TOK, 0), all_keys, all_values, None)
    blocks = lax.map(one_patch, jnp.arange(N_PATCH, dtype=jnp.int32))
    return blocks.reshape(TOKENS, HEADS * HD)

def cross_branch(queries, text_keys, text_values, mask_row):
    usable = (mask_row > 0)[None, None, :]

    def one_patch(patch_index):
        offset = patch_index * PATCH_TOK
        return softmax_mix(lax.dynamic_slice_in_dim(queries, offset, PATCH_TOK, 0), text_keys, text_values, usable)
    blocks = lax.map(one_patch, jnp.arange(N_PATCH, dtype=jnp.int32))
    return blocks.reshape(TOKENS, HEADS * HD)

def reference(fresh_query, fresh_key, fresh_value, stale_key, stale_value, cross_query, text_key, text_value, text_mask):
    self_parts = []
    cross_parts = []
    for branch in range(2):
        self_parts.append(self_branch(fresh_query[branch], fresh_key[branch], fresh_value[branch], stale_key[branch], stale_value[branch]))
        cross_parts.append(cross_branch(cross_query[branch], text_key[branch], text_value[branch], text_mask[branch]))
    return (jnp.stack(self_parts), jnp.stack(cross_parts))
```

```python
import functools
import math

import jax
import jax.numpy as jnp
from jax import lax
from jax.experimental import pallas as pl
from jax.experimental.pallas import tpu as pltpu
from jax.sharding import PartitionSpec as P

HD = 128
MESH = pl.DeviceIdType.MESH


def dot_nt(a, b):
    return lax.dot_general(a, b, (((1,), (1,)), ((), ())), preferred_element_type=jnp.float32)


def line_kernel(
    n_patch, n_head, nch,
    fq, fk, fv, sk, sv, cq, tk, tv, mask,
    so, co,
    fx, kv, txk, txv, mk, outs, outc,
    x_send, x_recv, x_loc, t_loc, kv_loc, own_send, fwd_send, kv_recv,
    o_send, o_recv, o_loc, c_send, c_recv, c_loc,
):
    p = lax.axis_index("patch")
    h = lax.axis_index("head")
    rows = fq.shape[1]
    prows = rows * n_head
    hcols = sk.shape[2]
    ccols = hcols // nch
    heads = hcols // HD
    cheads = heads // nch
    scale = 1.0 / math.sqrt(HD)
    fresh = (cq, fq, fk, fv)
    my_rows = pl.ds(pl.multiple_of(h * rows, rows), rows)

    for c in range(nch):
        for i, ref in enumerate((sk, sv)):
            pltpu.make_async_copy(
                ref.at[0, :, pl.ds(c * ccols, ccols)], kv.at[p, c, i], kv_loc.at[c, i]
            ).start()
    text_copies = [
        pltpu.make_async_copy(mask, mk, t_loc.at[0]),
        pltpu.make_async_copy(tk.at[0], txk, t_loc.at[1]),
        pltpu.make_async_copy(tv.at[0], txv, t_loc.at[2]),
    ]
    own_copies = [
        pltpu.make_async_copy(
            ref.at[0, :, pl.ds(pl.multiple_of(h * hcols, hcols), hcols)],
            fx.at[a, my_rows, :],
            x_loc.at[a],
        )
        for a, ref in enumerate(fresh)
    ]
    for cp in own_copies + text_copies:
        cp.start()

    barrier = pltpu.get_barrier_semaphore()
    has_right = p < n_patch - 1
    has_left = p > 0

    @pl.when(has_right)
    def _():
        pl.semaphore_signal(barrier, inc=1, device_id={"patch": p + 1}, device_id_type=MESH)

    @pl.when(has_left)
    def _():
        pl.semaphore_signal(barrier, inc=1, device_id={"patch": p - 1}, device_id_type=MESH)

    for k in range(1, n_head):
        pl.semaphore_signal(
            barrier, inc=1, device_id={"head": lax.rem(h + k, n_head)}, device_id_type=MESH
        )
    pl.semaphore_wait(
        barrier, n_head - 1 + has_right.astype(jnp.int32) + has_left.astype(jnp.int32)
    )

    def x_copy(a, k):
        peer = lax.rem(h + k, n_head)
        return pltpu.make_async_remote_copy(
            src_ref=fresh[a].at[0, :, pl.ds(pl.multiple_of(peer * hcols, hcols), hcols)],
            dst_ref=fx.at[a, my_rows, :],
            send_sem=x_send.at[a, k - 1],
            recv_sem=x_recv.at[a, k - 1],
            device_id={"head": peer},
            device_id_type=MESH,
        )

    def kv_copy(src, c, target, sem):
        return pltpu.make_async_remote_copy(
            src_ref=kv.at[src, c],
            dst_ref=kv.at[src, c],
            send_sem=sem,
            recv_sem=kv_recv.at[src, c],
            device_id={"patch": target},
            device_id_type=MESH,
        )

    def start_x():
        for a in (1, 0, 2, 3):
            for k in range(1, n_head):
                x_copy(a, k).start()

    def wait_own_kv(c):
        for i, ref in enumerate((sk, sv)):
            pltpu.make_async_copy(
                ref.at[0, :, pl.ds(c * ccols, ccols)], kv.at[p, c, i], kv_loc.at[c, i]
            ).wait()

    def wait_x(a):
        own_copies[a].wait()
        for k in range(1, n_head):
            x_copy(a, k).wait_recv()

    def out_copy(src, dst, c, k, send, recv):
        peer = lax.rem(h + k, n_head)
        return pltpu.make_async_remote_copy(
            src_ref=src.at[c, pl.ds(pl.multiple_of(peer * rows, rows), rows), :],
            dst_ref=dst.at[0, :, pl.ds(pl.multiple_of(h * hcols + c * ccols, HD), ccols)],
            send_sem=send.at[c, k - 1],
            recv_sem=recv.at[c, k - 1],
            device_id={"head": peer},
            device_id_type=MESH,
        )

    def local_out(src, dst, c, sem):
        return pltpu.make_async_copy(
            src.at[c, my_rows, :],
            dst.at[0, :, pl.ds(pl.multiple_of(h * hcols + c * ccols, HD), ccols)],
            sem.at[c],
        )

    def send_out(src, dst, c, send, recv, loc):
        for k in range(1, n_head):
            out_copy(src, dst, c, k, send, recv).start()
        local_out(src, dst, c, loc).start()

    def cross_chunk(c):
        usable = mk[...] > 0
        for i in range(cheads):
            cols = pl.ds((c * cheads + i) * HD, HD)
            scores = dot_nt(fx[0, :, cols], txk[:, cols]) * scale
            scores = jnp.where(usable, scores, -jnp.inf)
            top = jnp.max(scores, axis=-1, keepdims=True)
            weights = jnp.exp(scores - top)
            total = jnp.sum(weights, axis=-1, keepdims=True)
            mix = jnp.dot(
                weights.astype(jnp.bfloat16), txv[:, cols], preferred_element_type=jnp.float32
            )
            outc[c, :, i * HD : (i + 1) * HD] = (mix / total).astype(jnp.bfloat16)

    def query(j):
        return fx[1, :, pl.ds(j * HD, HD)]

    def weigh(q, keys, values, top=None):
        scores = dot_nt(q, keys) * scale
        new_top = jnp.max(scores, axis=-1, keepdims=True)
        if top is not None:
            new_top = jnp.maximum(top, new_top)
        weights = jnp.exp(scores - new_top).astype(jnp.bfloat16)
        wide = jnp.concatenate([values, jnp.ones_like(values)], axis=1)
        mixed = jnp.dot(weights, wide, preferred_element_type=jnp.float32)
        return new_top, mixed[:, HD:], mixed[:, :HD]

    def absorb_rows(state, q, keys, values):
        top, total, mix = state
        new_top, more_total, more_mix = weigh(q, keys, values, top)
        factor = jnp.exp(top - new_top)
        return new_top, total * factor + more_total, mix * factor + more_mix

    def kv_rows(i, j, *sources):
        c, k = divmod(j, cheads)
        parts = [kv[src, c, i, :, pl.ds(k * HD, HD)] for src in sources]
        return parts[0] if len(parts) == 1 else jnp.concatenate(parts, axis=0)

    def fresh_rows(i, j):
        return fx[2 + i, :, pl.ds(j * HD, HD)]

    def first(j):
        return weigh(query(j), fresh_rows(0, j), fresh_rows(1, j))

    def absorb(state, src, j):
        return absorb_rows(state, query(j), kv_rows(0, j, src), kv_rows(1, j, src))

    def line_program():
        start_x()
        for c in range(nch):
            wait_own_kv(c)

            @pl.when(has_right)
            def _():
                kv_copy(p, c, p + 1, own_send.at[0, c]).start()

            @pl.when(has_left)
            def _():
                kv_copy(p, c, p - 1, own_send.at[1, c]).start()

        shorter = jnp.minimum(p, n_patch - 1 - p)

        def slot_source(s):
            near = s // 2 + 1
            near_src = jnp.where(s % 2 == 0, p - near, p + near)
            far = s - shorter + 1
            far_src = jnp.where(p > shorter, p - far, p + far)
            return jnp.where(s < 2 * shorter, near_src, far_src)

        def forward_target(src):
            target = jnp.where(src < p, p + 1, p - 1)
            return target, (target >= 0) & (target < n_patch)

        def forward(s, c):
            src = slot_source(s)
            kv_copy(src, c, p, fwd_send.at[s, c]).wait_recv()
            target, valid = forward_target(src)

            @pl.when(valid)
            def _():
                kv_copy(src, c, target, fwd_send.at[s, c]).start()

        half = (nch + 1) // 2
        for cp in text_copies:
            cp.wait()
        wait_x(0)
        for c in range(half):
            cross_chunk(c)
        for c in range(half):
            forward(0, c)
        for c in range(half, nch):
            cross_chunk(c)
        for c in range(nch):
            send_out(outc, co, c, c_send, c_recv, c_loc)
        for c in range(half, nch):
            forward(0, c)
        for a in range(1, 4):
            wait_x(a)
        states = [first(j) for j in range(heads)]
        src = slot_source(0)
        states = [absorb(states[j], src, j) for j in range(heads)]

        def slot(s, states):
            src = slot_source(s)
            out = []
            for c in range(nch):
                forward(s, c)
                for j in range(c * cheads, (c + 1) * cheads):
                    out.append(absorb(states[j], src, j))
            return out

        if n_patch <= 8:
            for s in range(1, n_patch - 2):
                states = slot(s, states)
        else:
            states = lax.fori_loop(1, n_patch - 2, slot, states)
        last = n_patch - 2
        src = slot_source(last)
        for c in range(nch):
            if last > 0:
                forward(last, c)
            for i in range(cheads):
                j = c * cheads + i
                _, total, mix = absorb(states[j], src, j) if last > 0 else states[j]
                outs[c, :, i * HD : (i + 1) * HD] = (mix / total).astype(jnp.bfloat16)
            if c > 0:
                send_out(outs, so, c - 1, o_send, o_recv, o_loc)
        send_out(outs, so, nch - 1, o_send, o_recv, o_loc)

        for c in range(nch):

            @pl.when(has_right)
            def _():
                kv_copy(p, c, p + 1, own_send.at[0, c]).wait_send()

            @pl.when(has_left)
            def _():
                kv_copy(p, c, p - 1, own_send.at[1, c]).wait_send()

        def drain(s, carry):
            for c in range(nch):
                target, valid = forward_target(slot_source(s))

                @pl.when(valid)
                def _():
                    kv_copy(slot_source(s), c, target, fwd_send.at[s, c]).wait_send()

            return carry

        if n_patch <= 8:
            for s in range(n_patch - 1):
                drain(s, 0)
        else:
            lax.fori_loop(0, n_patch - 1, drain, 0)

    line_program()

    for a in range(4):
        for k in range(1, n_head):
            x_copy(a, k).wait_send()
    for src_ref, dst, send, recv, loc in (
        (outc, co, c_send, c_recv, c_loc),
        (outs, so, o_send, o_recv, o_loc),
    ):
        for c in range(nch):
            for k in range(1, n_head):
                cp = out_copy(src_ref, dst, c, k, send, recv)
                cp.wait_send()
                cp.wait_recv()
            local_out(src_ref, dst, c, loc).wait()


def line_attention(n_patch, n_head, *args):
    fq, fk, fv, sk, sv, cq, tk, tv, mask = args
    rows = fq.shape[1]
    prows = rows * n_head
    hcols = sk.shape[2]
    heads = hcols // HD
    nch = 2 if heads % 2 == 0 else 1
    ccols = hcols // nch
    txt = tk.shape[1]
    peers = max(n_head - 1, 1)
    any_spec = pl.BlockSpec(memory_space=pl.ANY)
    dma = pltpu.SemaphoreType.DMA
    bf16 = jnp.bfloat16
    mixed = pl.pallas_call(
        functools.partial(line_kernel, n_patch, n_head, nch),
        out_shape=(
            pltpu.VMEM(fq.shape, bf16),
            pltpu.VMEM(cq.shape, bf16),
        ),
        in_specs=[any_spec] * 9,
        out_specs=(pl.BlockSpec(memory_space=pltpu.VMEM),) * 2,
        scratch_shapes=[
            pltpu.VMEM((4, prows, hcols), bf16),
            pltpu.VMEM((n_patch, nch, 2, prows, ccols), bf16),
            pltpu.VMEM((txt, hcols), bf16),
            pltpu.VMEM((txt, hcols), bf16),
            pltpu.VMEM((1, txt), jnp.int32),
            pltpu.VMEM((nch, prows, ccols), bf16),
            pltpu.VMEM((nch, prows, ccols), bf16),
            dma((4, peers)),
            dma((4, peers)),
            dma((4,)),
            dma((3,)),
            dma((nch, 2)),
            dma((2, nch)),
            dma((n_patch, nch)),
            dma((n_patch, nch)),
            dma((nch, peers)),
            dma((nch, peers)),
            dma((nch,)),
            dma((nch, peers)),
            dma((nch, peers)),
            dma((nch,)),
        ],
        compiler_params=pltpu.CompilerParams(collective_id=0, has_side_effects=True),
        name="displaced_attention",
    )(*args)
    return mixed


END, ACROSS, FAR, OWN = range(4)
CQ, FQ, FK, FV = range(4)


def quad_kernel(
    n_head, nch,
    fq, fk, fv, sk, sv, cq, tk, tv, mask,
    so, co,
    fx, kv, tx, mk, dq, part, stat, outs, oute, outc,
    x_in, t_in, own_in, end_in, far_in, across_in, q_in, part_in, out_in, sent,
):
    p = lax.axis_index("patch")
    h = lax.axis_index("head")
    rows = fq.shape[1]
    prows = rows * n_head
    hcols = sk.shape[2]
    heads = hcols // HD
    cheads = heads // nch
    scale = 1.0 / math.sqrt(HD)
    fresh = (cq, fq, fk, fv)
    x_sem = (0, 1, 2, 2)
    across = 3 - p
    is_end = (p == 0) | (p == 3)
    inner = jnp.where(p < 2, 1, 2)
    outer = jnp.where(p < 2, 0, 3)
    my_rows = pl.ds(pl.multiple_of(h * rows, rows), rows)

    def head_cols(who):
        return pl.ds(pl.multiple_of(who * hcols, hcols), hcols)

    def cols(c):
        return pl.ds(c * cheads * HD, cheads * HD)

    def own_copy(a):
        return pltpu.make_async_copy(
            fresh[a].at[0, :, head_cols(h)], fx.at[a, my_rows, :], x_in.at[x_sem[a]]
        )

    def remote(src, dst, send, recv, **to):
        return pltpu.make_async_remote_copy(
            src_ref=src, dst_ref=dst, send_sem=send, recv_sem=recv,
            device_id=to, device_id_type=MESH,
        )

    def wait_bytes(ref, sem):
        pltpu.make_async_copy(ref, ref, sem).wait()

    def load_text():
        pltpu.make_async_copy(mask, mk, t_in.at[0]).start()
        pltpu.make_async_copy(tk.at[0], tx.at[0], t_in.at[1]).start()
        pltpu.make_async_copy(tv.at[0], tx.at[1], t_in.at[1]).start()

    barrier = pltpu.get_barrier_semaphore()
    for k in range(1, n_head):
        pl.semaphore_signal(
            barrier, inc=1, device_id={"head": lax.rem(h + k, n_head)}, device_id_type=MESH
        )

    @pl.when(is_end)
    def _():
        pl.semaphore_signal(barrier, inc=1, device_id={"patch": inner}, device_id_type=MESH)

    @pl.when(jnp.logical_not(is_end))
    def _():
        pl.semaphore_signal(barrier, inc=1, device_id={"patch": across}, device_id_type=MESH)
        pl.semaphore_signal(barrier, inc=1, device_id={"patch": outer}, device_id_type=MESH)
        for i, ref in enumerate((sk, sv)):
            pltpu.make_async_copy(ref.at[0], kv.at[OWN, i], own_in.at[0]).start()

    for a in range(4):
        own_copy(a).start()
    load_text()
    pl.semaphore_wait(barrier, n_head - 1 + jnp.where(is_end, 1, 2))

    def send_x(a):
        for k in range(1, n_head):
            peer = lax.rem(h + k, n_head)
            remote(
                fresh[a].at[0, :, head_cols(peer)], fx.at[a, my_rows, :],
                sent.at[0], x_in.at[x_sem[a]], head=peer,
            ).start()

    def scores_of(q, keys):
        return dot_nt(q, keys) * scale

    def mix_of(weights, values):
        wide = jnp.concatenate([values, jnp.ones_like(values)], axis=1)
        mixed = jnp.dot(
            weights.astype(jnp.bfloat16), wide, preferred_element_type=jnp.float32
        )
        return mixed[:, :HD], mixed[:, HD:]

    def cross_heads(first, last):
        usable = mk[...] > 0
        for j in range(first, last):
            at = slice(j * HD, (j + 1) * HD)
            scores = jnp.where(usable, scores_of(fx[CQ, :, at], tx[0, :, at]), -jnp.inf)
            weights = jnp.exp(scores - jnp.max(scores, axis=-1, keepdims=True))
            total = jnp.sum(weights, axis=-1, keepdims=True)
            mix = jnp.dot(
                weights.astype(jnp.bfloat16), tx[1, :, at], preferred_element_type=jnp.float32
            )
            outc[:, at] = (mix / total).astype(jnp.bfloat16)

    def send_out(src, dst, at, size, send, recv):
        dst_at = dst.at[0, :, pl.ds(pl.multiple_of(h * hcols + at, HD), size)]
        for k in range(1, n_head):
            peer = lax.rem(h + k, n_head)
            remote(
                src.at[pl.ds(pl.multiple_of(peer * rows, rows), rows), pl.ds(at, size)],
                dst_at, send, recv, head=peer,
            ).start()
        pltpu.make_async_copy(src.at[my_rows, pl.ds(at, size)], dst_at, recv).start()

    def send_cross():
        send_out(outc, co, 0, hcols, sent.at[1], out_in.at[1])

    def wait_text():
        wait_bytes(mk, t_in.at[0])
        wait_bytes(tx, t_in.at[1])

    def end_program():
        def send_kv(c):
            for i, ref in enumerate((sk, sv)):
                remote(
                    ref.at[0, :, cols(c)], kv.at[END, i, :, cols(c)],
                    sent.at[2], end_in.at[c], patch=inner,
                ).start()

        lead = (nch + 1) // 2
        send_x(FQ)
        send_kv(0)
        send_x(FK)
        send_x(FV)
        send_x(CQ)
        for c in range(1, lead):
            send_kv(c)
        wait_bytes(fx.at[FQ], x_in.at[1])
        remote(fx.at[FQ], dq, sent.at[3], q_in.at[0], patch=inner).start()
        for c in range(lead, nch):
            send_kv(c)
        wait_bytes(fx.at[pl.ds(FK, 2)], x_in.at[2])
        lanes = lax.broadcasted_iota(jnp.int32, (prows, HD), 1)
        lse = jnp.zeros((prows, HD), jnp.float32)
        for j in range(heads):
            at = slice(j * HD, (j + 1) * HD)
            scores = scores_of(fx[FQ, :, at], fx[FK, :, at])
            top = jnp.max(scores, axis=-1, keepdims=True)
            mix, total = mix_of(jnp.exp(scores - top), fx[FV, :, at])
            outs[:, at] = (mix / total).astype(jnp.bfloat16)
            lse = jnp.where(lanes == j, top + jnp.log(total), lse)
        stat[1] = lse
        remote(outs, part, sent.at[4], part_in.at[0], patch=inner).start()
        remote(stat.at[1], stat.at[0], sent.at[5], part_in.at[1], patch=inner).start()
        wait_text()
        wait_bytes(fx.at[CQ], x_in.at[0])
        cross_heads(0, heads)
        send_cross()
        wait_bytes(kv.at[END], sent.at[2])
        wait_bytes(dq, sent.at[3])
        wait_bytes(part, sent.at[4])
        wait_bytes(stat.at[0], sent.at[5])

    def middle_program():
        for i, ref in enumerate((sk, sv)):
            remote(
                ref.at[0], kv.at[ACROSS, i], sent.at[2], across_in.at[0], patch=across
            ).start()
        for a in (CQ, FQ, FK, FV):
            send_x(a)

        def pass_on(c):
            src = kv.at[END, :, :, cols(c)]
            wait_bytes(src, end_in.at[c])
            remote(
                src, kv.at[FAR, :, :, cols(c)], sent.at[3], far_in.at[c], patch=across
            ).start()

        pass_on(0)
        wait_text()
        wait_bytes(fx.at[CQ], x_in.at[0])
        half = heads // 2
        cross_heads(0, half)
        if nch > 1:
            pass_on(1)
        cross_heads(half, heads)
        send_cross()
        for c in range(2, nch):
            pass_on(c)
        wait_bytes(fx.at[FQ], x_in.at[1])
        wait_bytes(fx.at[pl.ds(FK, 2)], x_in.at[2])
        wait_bytes(kv.at[OWN], own_in.at[0])
        wait_bytes(kv.at[ACROSS], across_in.at[0])
        wait_bytes(dq, q_in.at[0])
        wait_bytes(part, part_in.at[0])
        wait_bytes(stat.at[0], part_in.at[1])
        for c in range(nch):
            wait_bytes(kv.at[FAR, :, :, cols(c)], far_in.at[c])
            for j in range(c * cheads, (c + 1) * cheads):
                at = slice(j * HD, (j + 1) * HD)
                shared = [[kv[s, i, :, at] for s in (ACROSS, FAR)] for i in range(2)]
                keys = jnp.concatenate([kv[OWN, 0, :, at]] + shared[0], axis=0)
                values = jnp.concatenate([kv[OWN, 1, :, at]] + shared[1], axis=0)
                scores = scores_of(dq[:, at], keys)
                lse = stat[0, :, j : j + 1]
                top = jnp.maximum(jnp.max(scores, axis=-1, keepdims=True), lse)
                mix, total = mix_of(jnp.exp(scores - top), values)
                theirs = jnp.exp(lse - top)
                mix = mix + part[:, at].astype(jnp.float32) * theirs
                oute[:, at] = (mix / (total + theirs)).astype(jnp.bfloat16)
                keys = jnp.concatenate([fx[FK, :, at], kv[END, 0, :, at]] + shared[0], axis=0)
                values = jnp.concatenate([fx[FV, :, at], kv[END, 1, :, at]] + shared[1], axis=0)
                scores = scores_of(fx[FQ, :, at], keys)
                top = jnp.max(scores, axis=-1, keepdims=True)
                mix, total = mix_of(jnp.exp(scores - top), values)
                outs[:, at] = (mix / total).astype(jnp.bfloat16)
            size = cheads * HD
            first = c * size
            dst = so.at[0, :, pl.ds(pl.multiple_of(h * hcols + first, HD), size)]
            for k in range(n_head - 1, -1, -1):
                to = lax.rem(h + k, n_head)
                remote(
                    oute.at[pl.ds(pl.multiple_of(to * rows, rows), rows), pl.ds(first, size)],
                    dst, sent.at[4], out_in.at[0], patch=outer, head=to,
                ).start()
            send_out(outs, so, first, size, sent.at[5], out_in.at[0])
        wait_bytes(kv.at[ACROSS], sent.at[2])
        wait_bytes(kv.at[FAR], sent.at[3])
        wait_bytes(oute, sent.at[4])
        if n_head > 1:
            wait_bytes(outs.at[pl.ds(0, rows * (n_head - 1)), :], sent.at[5])

    pl.when(is_end)(end_program)
    pl.when(jnp.logical_not(is_end))(middle_program)
    if n_head > 1:
        wait_bytes(fx.at[:, pl.ds(0, rows * (n_head - 1)), :], sent.at[0])
        wait_bytes(outc.at[pl.ds(0, rows * (n_head - 1)), :], sent.at[1])
    wait_bytes(co, out_in.at[1])
    wait_bytes(so, out_in.at[0])


def quad_attention(n_head, *args):
    fq, fk, fv, sk, sv, cq, tk, tv, mask = args
    prows = fq.shape[1] * n_head
    hcols = sk.shape[2]
    heads = hcols // HD
    nch = next(n for n in (5, 4, 3, 2, 1) if heads % n == 0)
    txt = tk.shape[1]
    dma = pltpu.SemaphoreType.DMA
    bf16 = jnp.bfloat16
    patch = pltpu.VMEM((prows, hcols), bf16)
    return pl.pallas_call(
        functools.partial(quad_kernel, n_head, nch),
        out_shape=(pltpu.VMEM(fq.shape, bf16), pltpu.VMEM(cq.shape, bf16)),
        in_specs=[pl.BlockSpec(memory_space=pl.ANY)] * 9,
        out_specs=(pl.BlockSpec(memory_space=pltpu.VMEM),) * 2,
        scratch_shapes=[
            pltpu.VMEM((4, prows, hcols), bf16),
            pltpu.VMEM((4, 2, prows, hcols), bf16),
            pltpu.VMEM((2, txt, hcols), bf16),
            pltpu.VMEM((1, txt), jnp.int32),
            patch,
            patch,
            pltpu.VMEM((2, prows, HD), jnp.float32),
            patch,
            patch,
            patch,
            dma((3,)),
            dma((2,)),
            dma((1,)),
            dma((nch,)),
            dma((nch,)),
            dma((1,)),
            dma((1,)),
            dma((2,)),
            dma((2,)),
            dma((6,)),
        ],
        compiler_params=pltpu.CompilerParams(collective_id=0, has_side_effects=True),
        name="displaced_attention",
    )(*args)


def store_kernel(a, b, so, co, sem):
    copies = [
        pltpu.make_async_copy(a, so, sem.at[0]),
        pltpu.make_async_copy(b, co, sem.at[1]),
    ]
    for cp in copies:
        cp.start()
    for cp in copies:
        cp.wait()


def store(a, b):
    return pl.pallas_call(
        store_kernel,
        out_shape=(
            jax.ShapeDtypeStruct(a.shape, a.dtype),
            jax.ShapeDtypeStruct(b.shape, b.dtype),
        ),
        in_specs=[pl.BlockSpec(memory_space=pltpu.VMEM)] * 2,
        out_specs=(pl.BlockSpec(memory_space=pltpu.HBM),) * 2,
        scratch_shapes=[pltpu.SemaphoreType.DMA((2,))],
        compiler_params=pltpu.CompilerParams(vmem_limit_bytes=1024 * 1024),
        name="store_outputs",
    )(a, b)


def per_device(n_patch, n_head, *args):
    if n_patch == 4:
        return store(*quad_attention(n_head, *args))
    return store(*line_attention(n_patch, n_head, *args))


def solution(mesh):
    return jax.shard_map(
        functools.partial(per_device, mesh.shape["patch"], mesh.shape["head"]),
        mesh=mesh,
        in_specs=(
            P(("group", "cfg"), ("patch", "head"), None),
            P(("group", "cfg"), ("patch", "head"), None),
            P(("group", "cfg"), ("patch", "head"), None),
            P(("group", "cfg"), "patch", "head"),
            P(("group", "cfg"), "patch", "head"),
            P(("group", "cfg"), ("patch", "head"), None),
            P(("group", "cfg"), None, "head"),
            P(("group", "cfg"), None, "head"),
            P(("group", "cfg"), None),
        ),
        out_specs=(
            P(("group", "cfg"), ("patch", "head"), None),
            P(("group", "cfg"), ("patch", "head"), None),
        ),
        check_vma=False,
    )
```

```python
import functools
import math

import jax
import jax.numpy as jnp
from jax import lax
from jax.experimental import pallas as pl
from jax.experimental.pallas import tpu as pltpu
from jax.sharding import PartitionSpec as P

HD = 128
MESH = pl.DeviceIdType.MESH


def dot_nt(a, b):
    return lax.dot_general(a, b, (((1,), (1,)), ((), ())), preferred_element_type=jnp.float32)


def line_kernel(
    n_patch, n_head, nch,
    fq, fk, fv, sk, sv, cq, tk, tv, mask,
    so, co,
    fx, kv, txk, txv, mk, outs, outc,
    x_send, x_recv, x_loc, t_loc, kv_loc, own_send, fwd_send, kv_recv,
    o_send, o_recv, o_loc, c_send, c_recv, c_loc,
):
    p = lax.axis_index("patch")
    h = lax.axis_index("head")
    rows = fq.shape[1]
    prows = rows * n_head
    hcols = sk.shape[2]
    ccols = hcols // nch
    heads = hcols // HD
    cheads = heads // nch
    scale = 1.0 / math.sqrt(HD)
    fresh = (cq, fq, fk, fv)
    my_rows = pl.ds(pl.multiple_of(h * rows, rows), rows)

    for c in range(nch):
        for i, ref in enumerate((sk, sv)):
            pltpu.make_async_copy(
                ref.at[0, :, pl.ds(c * ccols, ccols)], kv.at[p, c, i], kv_loc.at[c, i]
            ).start()
    text_copies = [
        pltpu.make_async_copy(mask, mk, t_loc.at[0]),
        pltpu.make_async_copy(tk.at[0], txk, t_loc.at[1]),
        pltpu.make_async_copy(tv.at[0], txv, t_loc.at[2]),
    ]
    own_copies = [
        pltpu.make_async_copy(
            ref.at[0, :, pl.ds(pl.multiple_of(h * hcols, hcols), hcols)],
            fx.at[a, my_rows, :],
            x_loc.at[a],
        )
        for a, ref in enumerate(fresh)
    ]
    for cp in own_copies + text_copies:
        cp.start()

    barrier = pltpu.get_barrier_semaphore()
    has_right = p < n_patch - 1
    has_left = p > 0

    @pl.when(has_right)
    def _():
        pl.semaphore_signal(barrier, inc=1, device_id={"patch": p + 1}, device_id_type=MESH)

    @pl.when(has_left)
    def _():
        pl.semaphore_signal(barrier, inc=1, device_id={"patch": p - 1}, device_id_type=MESH)

    for k in range(1, n_head):
        pl.semaphore_signal(
            barrier, inc=1, device_id={"head": lax.rem(h + k, n_head)}, device_id_type=MESH
        )
    pl.semaphore_wait(
        barrier, n_head - 1 + has_right.astype(jnp.int32) + has_left.astype(jnp.int32)
    )

    def x_copy(a, k):
        peer = lax.rem(h + k, n_head)
        return pltpu.make_async_remote_copy(
            src_ref=fresh[a].at[0, :, pl.ds(pl.multiple_of(peer * hcols, hcols), hcols)],
            dst_ref=fx.at[a, my_rows, :],
            send_sem=x_send.at[a, k - 1],
            recv_sem=x_recv.at[a, k - 1],
            device_id={"head": peer},
            device_id_type=MESH,
        )

    def kv_copy(src, c, target, sem):
        return pltpu.make_async_remote_copy(
            src_ref=kv.at[src, c],
            dst_ref=kv.at[src, c],
            send_sem=sem,
            recv_sem=kv_recv.at[src, c],
            device_id={"patch": target},
            device_id_type=MESH,
        )

    def start_x():
        for a in (1, 0, 2, 3):
            for k in range(1, n_head):
                x_copy(a, k).start()

    def wait_own_kv(c):
        for i, ref in enumerate((sk, sv)):
            pltpu.make_async_copy(
                ref.at[0, :, pl.ds(c * ccols, ccols)], kv.at[p, c, i], kv_loc.at[c, i]
            ).wait()

    def wait_x(a):
        own_copies[a].wait()
        for k in range(1, n_head):
            x_copy(a, k).wait_recv()

    def out_copy(src, dst, c, k, send, recv):
        peer = lax.rem(h + k, n_head)
        return pltpu.make_async_remote_copy(
            src_ref=src.at[c, pl.ds(pl.multiple_of(peer * rows, rows), rows), :],
            dst_ref=dst.at[0, :, pl.ds(pl.multiple_of(h * hcols + c * ccols, HD), ccols)],
            send_sem=send.at[c, k - 1],
            recv_sem=recv.at[c, k - 1],
            device_id={"head": peer},
            device_id_type=MESH,
        )

    def local_out(src, dst, c, sem):
        return pltpu.make_async_copy(
            src.at[c, my_rows, :],
            dst.at[0, :, pl.ds(pl.multiple_of(h * hcols + c * ccols, HD), ccols)],
            sem.at[c],
        )

    def send_out(src, dst, c, send, recv, loc):
        for k in range(1, n_head):
            out_copy(src, dst, c, k, send, recv).start()
        local_out(src, dst, c, loc).start()

    def cross_chunk(c):
        usable = mk[...] > 0
        for i in range(cheads):
            cols = pl.ds((c * cheads + i) * HD, HD)
            scores = dot_nt(fx[0, :, cols], txk[:, cols]) * scale
            scores = jnp.where(usable, scores, -jnp.inf)
            top = jnp.max(scores, axis=-1, keepdims=True)
            weights = jnp.exp(scores - top)
            total = jnp.sum(weights, axis=-1, keepdims=True)
            mix = jnp.dot(
                weights.astype(jnp.bfloat16), txv[:, cols], preferred_element_type=jnp.float32
            )
            outc[c, :, i * HD : (i + 1) * HD] = (mix / total).astype(jnp.bfloat16)

    def query(j):
        return fx[1, :, pl.ds(j * HD, HD)]

    def weigh(q, keys, values, top=None):
        scores = dot_nt(q, keys) * scale
        new_top = jnp.max(scores, axis=-1, keepdims=True)
        if top is not None:
            new_top = jnp.maximum(top, new_top)
        weights = jnp.exp(scores - new_top).astype(jnp.bfloat16)
        wide = jnp.concatenate([values, jnp.ones_like(values)], axis=1)
        mixed = jnp.dot(weights, wide, preferred_element_type=jnp.float32)
        return new_top, mixed[:, HD:], mixed[:, :HD]

    def absorb_rows(state, q, keys, values):
        top, total, mix = state
        new_top, more_total, more_mix = weigh(q, keys, values, top)
        factor = jnp.exp(top - new_top)
        return new_top, total * factor + more_total, mix * factor + more_mix

    def kv_rows(i, j, *sources):
        c, k = divmod(j, cheads)
        parts = [kv[src, c, i, :, pl.ds(k * HD, HD)] for src in sources]
        return parts[0] if len(parts) == 1 else jnp.concatenate(parts, axis=0)

    def fresh_rows(i, j):
        return fx[2 + i, :, pl.ds(j * HD, HD)]

    def first(j):
        return weigh(query(j), fresh_rows(0, j), fresh_rows(1, j))

    def absorb(state, src, j):
        return absorb_rows(state, query(j), kv_rows(0, j, src), kv_rows(1, j, src))

    def line_program():
        start_x()
        for c in range(nch):
            wait_own_kv(c)

            @pl.when(has_right)
            def _():
                kv_copy(p, c, p + 1, own_send.at[0, c]).start()

            @pl.when(has_left)
            def _():
                kv_copy(p, c, p - 1, own_send.at[1, c]).start()

        shorter = jnp.minimum(p, n_patch - 1 - p)

        def slot_source(s):
            near = s // 2 + 1
            near_src = jnp.where(s % 2 == 0, p - near, p + near)
            far = s - shorter + 1
            far_src = jnp.where(p > shorter, p - far, p + far)
            return jnp.where(s < 2 * shorter, near_src, far_src)

        def forward_target(src):
            target = jnp.where(src < p, p + 1, p - 1)
            return target, (target >= 0) & (target < n_patch)

        def forward(s, c):
            src = slot_source(s)
            kv_copy(src, c, p, fwd_send.at[s, c]).wait_recv()
            target, valid = forward_target(src)

            @pl.when(valid)
            def _():
                kv_copy(src, c, target, fwd_send.at[s, c]).start()

        half = (nch + 1) // 2
        for cp in text_copies:
            cp.wait()
        wait_x(0)
        for c in range(half):
            cross_chunk(c)
        for c in range(half):
            forward(0, c)
        for c in range(half, nch):
            cross_chunk(c)
        for c in range(nch):
            send_out(outc, co, c, c_send, c_recv, c_loc)
        for c in range(half, nch):
            forward(0, c)
        for a in range(1, 4):
            wait_x(a)
        states = [first(j) for j in range(heads)]
        src = slot_source(0)
        states = [absorb(states[j], src, j) for j in range(heads)]

        def slot(s, states):
            src = slot_source(s)
            out = []
            for c in range(nch):
                forward(s, c)
                for j in range(c * cheads, (c + 1) * cheads):
                    out.append(absorb(states[j], src, j))
            return out

        if n_patch <= 8:
            for s in range(1, n_patch - 2):
                states = slot(s, states)
        else:
            states = lax.fori_loop(1, n_patch - 2, slot, states)
        last = n_patch - 2
        src = slot_source(last)
        for c in range(nch):
            if last > 0:
                forward(last, c)
            for i in range(cheads):
                j = c * cheads + i
                _, total, mix = absorb(states[j], src, j) if last > 0 else states[j]
                outs[c, :, i * HD : (i + 1) * HD] = (mix / total).astype(jnp.bfloat16)
            if c > 0:
                send_out(outs, so, c - 1, o_send, o_recv, o_loc)
        send_out(outs, so, nch - 1, o_send, o_recv, o_loc)

        for c in range(nch):

            @pl.when(has_right)
            def _():
                kv_copy(p, c, p + 1, own_send.at[0, c]).wait_send()

            @pl.when(has_left)
            def _():
                kv_copy(p, c, p - 1, own_send.at[1, c]).wait_send()

        def drain(s, carry):
            for c in range(nch):
                target, valid = forward_target(slot_source(s))

                @pl.when(valid)
                def _():
                    kv_copy(slot_source(s), c, target, fwd_send.at[s, c]).wait_send()

            return carry

        if n_patch <= 8:
            for s in range(n_patch - 1):
                drain(s, 0)
        else:
            lax.fori_loop(0, n_patch - 1, drain, 0)

    line_program()

    for a in range(4):
        for k in range(1, n_head):
            x_copy(a, k).wait_send()
    for src_ref, dst, send, recv, loc in (
        (outc, co, c_send, c_recv, c_loc),
        (outs, so, o_send, o_recv, o_loc),
    ):
        for c in range(nch):
            for k in range(1, n_head):
                cp = out_copy(src_ref, dst, c, k, send, recv)
                cp.wait_send()
                cp.wait_recv()
            local_out(src_ref, dst, c, loc).wait()


def line_attention(n_patch, n_head, *args):
    fq, fk, fv, sk, sv, cq, tk, tv, mask = args
    rows = fq.shape[1]
    prows = rows * n_head
    hcols = sk.shape[2]
    heads = hcols // HD
    nch = 2 if heads % 2 == 0 else 1
    ccols = hcols // nch
    txt = tk.shape[1]
    peers = max(n_head - 1, 1)
    any_spec = pl.BlockSpec(memory_space=pl.ANY)
    dma = pltpu.SemaphoreType.DMA
    bf16 = jnp.bfloat16
    mixed = pl.pallas_call(
        functools.partial(line_kernel, n_patch, n_head, nch),
        out_shape=(
            pltpu.VMEM(fq.shape, bf16),
            pltpu.VMEM(cq.shape, bf16),
        ),
        in_specs=[any_spec] * 9,
        out_specs=(pl.BlockSpec(memory_space=pltpu.VMEM),) * 2,
        scratch_shapes=[
            pltpu.VMEM((4, prows, hcols), bf16),
            pltpu.VMEM((n_patch, nch, 2, prows, ccols), bf16),
            pltpu.VMEM((txt, hcols), bf16),
            pltpu.VMEM((txt, hcols), bf16),
            pltpu.VMEM((1, txt), jnp.int32),
            pltpu.VMEM((nch, prows, ccols), bf16),
            pltpu.VMEM((nch, prows, ccols), bf16),
            dma((4, peers)),
            dma((4, peers)),
            dma((4,)),
            dma((3,)),
            dma((nch, 2)),
            dma((2, nch)),
            dma((n_patch, nch)),
            dma((n_patch, nch)),
            dma((nch, peers)),
            dma((nch, peers)),
            dma((nch,)),
            dma((nch, peers)),
            dma((nch, peers)),
            dma((nch,)),
        ],
        compiler_params=pltpu.CompilerParams(collective_id=0, has_side_effects=True),
        name="displaced_attention",
    )(*args)
    return mixed


END, ACROSS, FAR, OWN = range(4)
CQ, FQ, FK, FV = range(4)
DIRECT = 3


def chunk_sizes(heads):
    size = max(1, heads // 5)
    whole = (heads - 1) // size
    return [size] * whole + [1] * (heads - whole * size)


def quad_kernel(
    n_head, direct,
    fq, fk, fv, sk, sv, cq, tk, tv, mask,
    so, co,
    fx, kv, tx, mk, dq, part, stat, outs, oute, outc,
    x_in, t_in, own_in, end_in, far_in, across_in, q_in, part_in, out_in, sent,
):
    p = lax.axis_index("patch")
    h = lax.axis_index("head")
    rows = fq.shape[1]
    prows = rows * n_head
    hcols = sk.shape[2]
    heads = hcols // HD
    sizes = chunk_sizes(heads)
    nch = len(sizes)
    starts = [sum(sizes[:c]) for c in range(nch + 1)]
    early = slice(0, starts[direct] * HD)
    late = slice(starts[direct] * HD, hcols)
    scale = 1.0 / math.sqrt(HD)
    fresh = (cq, fq, fk, fv)
    x_sem = (0, 1, 2, 2)
    across = 3 - p
    is_end = (p == 0) | (p == 3)
    inner = jnp.where(p < 2, 1, 2)
    outer = jnp.where(p < 2, 0, 3)
    my_rows = pl.ds(pl.multiple_of(h * rows, rows), rows)

    def head_cols(who):
        return pl.ds(pl.multiple_of(who * hcols, hcols), hcols)

    def cols(c):
        return slice(starts[c] * HD, starts[c + 1] * HD)

    def own_copy(a):
        return pltpu.make_async_copy(
            fresh[a].at[0, :, head_cols(h)], fx.at[a, my_rows, :], x_in.at[x_sem[a]]
        )

    def remote(src, dst, send, recv, **to):
        return pltpu.make_async_remote_copy(
            src_ref=src, dst_ref=dst, send_sem=send, recv_sem=recv,
            device_id=to, device_id_type=MESH,
        )

    def wait_bytes(ref, sem):
        pltpu.make_async_copy(ref, ref, sem).wait()

    def load_text():
        pltpu.make_async_copy(mask, mk, t_in.at[0]).start()
        pltpu.make_async_copy(tk.at[0], tx.at[0], t_in.at[1]).start()
        pltpu.make_async_copy(tv.at[0], tx.at[1], t_in.at[1]).start()

    barrier = pltpu.get_barrier_semaphore()
    for k in range(1, n_head):
        pl.semaphore_signal(
            barrier, inc=1, device_id={"head": lax.rem(h + k, n_head)}, device_id_type=MESH
        )

    @pl.when(is_end)
    def _():
        pl.semaphore_signal(barrier, inc=1, device_id={"patch": inner}, device_id_type=MESH)

    @pl.when(jnp.logical_not(is_end))
    def _():
        pl.semaphore_signal(barrier, inc=1, device_id={"patch": across}, device_id_type=MESH)
        pl.semaphore_signal(barrier, inc=1, device_id={"patch": outer}, device_id_type=MESH)
        for i, ref in enumerate((sk, sv)):
            pltpu.make_async_copy(ref.at[0], kv.at[OWN, i], own_in.at[0]).start()

    for a in range(4):
        own_copy(a).start()
    load_text()
    pl.semaphore_wait(barrier, n_head - 1 + jnp.where(is_end, 1, 2))

    def send_x(a):
        for k in range(1, n_head):
            peer = lax.rem(h + k, n_head)
            remote(
                fresh[a].at[0, :, head_cols(peer)], fx.at[a, my_rows, :],
                sent.at[0], x_in.at[x_sem[a]], head=peer,
            ).start()

    def scores_of(q, keys):
        return dot_nt(q, keys) * scale

    def mix_of(weights, values):
        wide = jnp.concatenate([values, jnp.ones_like(values)], axis=1)
        mixed = jnp.dot(
            weights.astype(jnp.bfloat16), wide, preferred_element_type=jnp.float32
        )
        return mixed[:, :HD], mixed[:, HD:]

    def attend_own(c):
        for j in range(starts[c], starts[c + 1]):
            at = slice(j * HD, (j + 1) * HD)
            keys, values = (
                jnp.concatenate([fx[FK + i, :, at]] + [kv[s, i, :, at] for s in (END, ACROSS, FAR)])
                for i in range(2)
            )
            scores = scores_of(fx[FQ, :, at], keys)
            mix, total = mix_of(jnp.exp(scores - jnp.max(scores, axis=-1, keepdims=True)), values)
            outs[:, at] = (mix / total).astype(jnp.bfloat16)

    def attend_end(c):
        for j in range(starts[c], starts[c + 1]):
            at = slice(j * HD, (j + 1) * HD)
            keys, values = (
                jnp.concatenate([kv[s, i, :, at] for s in (OWN, ACROSS, FAR)]) for i in range(2)
            )
            scores = scores_of(dq[:, at], keys)
            lse = stat[0, :, j : j + 1]
            top = jnp.maximum(jnp.max(scores, axis=-1, keepdims=True), lse)
            mix, total = mix_of(jnp.exp(scores - top), values)
            theirs = jnp.exp(lse - top)
            mix = mix + part[:, at].astype(jnp.float32) * theirs
            oute[:, at] = (mix / (total + theirs)).astype(jnp.bfloat16)

    def cross_heads(first, last):
        usable = mk[...] > 0
        for j in range(first, last):
            at = slice(j * HD, (j + 1) * HD)
            scores = jnp.where(usable, scores_of(fx[CQ, :, at], tx[0, :, at]), -jnp.inf)
            weights = jnp.exp(scores - jnp.max(scores, axis=-1, keepdims=True))
            total = jnp.sum(weights, axis=-1, keepdims=True)
            mix = jnp.dot(
                weights.astype(jnp.bfloat16), tx[1, :, at], preferred_element_type=jnp.float32
            )
            outc[:, at] = (mix / total).astype(jnp.bfloat16)

    def out_at(dst, at):
        return dst.at[0, :, pl.ds(pl.multiple_of(h * hcols + at.start, HD), at.stop - at.start)]

    def rows_of(src, who, at):
        return src.at[pl.ds(pl.multiple_of(who * rows, rows), rows), at]

    def send_out(src, dst, at, send, recv):
        for k in range(1, n_head):
            peer = lax.rem(h + k, n_head)
            remote(rows_of(src, peer, at), out_at(dst, at), send, recv, head=peer).start()
        pltpu.make_async_copy(rows_of(src, h, at), out_at(dst, at), recv).start()

    def wait_peers(src, at, send):
        if n_head > 1:
            wait_bytes(src.at[pl.ds(0, rows * (n_head - 1)), at], send)

    def send_cross():
        send_out(outc, co, slice(0, hcols), sent.at[1], out_in.at[1])

    def wait_text():
        wait_bytes(mk, t_in.at[0])
        wait_bytes(tx, t_in.at[1])

    def end_program():
        def send_kv(c):
            for i, ref in enumerate((sk, sv)):
                remote(
                    ref.at[0, :, cols(c)], kv.at[END, i, :, cols(c)],
                    sent.at[2], end_in.at[c], patch=inner,
                ).start()

        lead = (nch + 1) // 2
        send_x(FQ)
        send_kv(0)
        send_x(FK)
        send_x(FV)
        send_x(CQ)
        for c in range(1, lead):
            send_kv(c)
        wait_bytes(fx.at[FQ], x_in.at[1])
        remote(
            fx.at[FQ, :, late], dq.at[:, late], sent.at[3], q_in.at[0], patch=inner
        ).start()
        for c in range(lead, nch):
            send_kv(c)
        wait_bytes(fx.at[pl.ds(FK, 2)], x_in.at[2])
        lanes = lax.broadcasted_iota(jnp.int32, (prows, HD), 1)
        lse = jnp.zeros((prows, HD), jnp.float32)
        for j in range(starts[direct], heads):
            at = slice(j * HD, (j + 1) * HD)
            scores = scores_of(fx[FQ, :, at], fx[FK, :, at])
            top = jnp.max(scores, axis=-1, keepdims=True)
            mix, total = mix_of(jnp.exp(scores - top), fx[FV, :, at])
            outs[:, at] = (mix / total).astype(jnp.bfloat16)
            lse = jnp.where(lanes == j, top + jnp.log(total), lse)
        stat[1] = lse
        remote(
            outs.at[:, late], part.at[:, late], sent.at[4], part_in.at[0], patch=inner
        ).start()
        remote(stat.at[1], stat.at[0], sent.at[5], part_in.at[1], patch=inner).start()
        wait_text()
        wait_bytes(fx.at[CQ], x_in.at[0])
        cross_heads(0, heads)
        send_cross()
        for c in range(direct):
            wait_bytes(kv.at[pl.ds(END, 3), :, :, cols(c)], far_in.at[c])
            attend_own(c)
            send_out(outs, so, cols(c), sent.at[6], out_in.at[0])
        wait_bytes(kv.at[END], sent.at[2])
        wait_bytes(dq.at[:, late], sent.at[3])
        wait_bytes(part.at[:, late], sent.at[4])
        wait_bytes(stat.at[0], sent.at[5])
        if direct:
            wait_peers(outs, early, sent.at[6])

    def middle_program():
        def send_own(at, recv):
            for i, ref in enumerate((sk, sv)):
                remote(
                    ref.at[0, :, at], kv.at[ACROSS, i, :, at], sent.at[2], recv, patch=across
                ).start()

        def pass_out(src, slot, c):
            remote(
                src, kv.at[slot, :, :, cols(c)], sent.at[6], far_in.at[c], patch=outer
            ).start()

        def pass_across(c):
            src = kv.at[END, :, :, cols(c)]
            wait_bytes(src, end_in.at[c])
            remote(
                src, kv.at[FAR, :, :, cols(c)], sent.at[3], far_in.at[c], patch=across
            ).start()

        if direct:
            send_own(early, across_in.at[0])
        send_own(late, across_in.at[1])
        for a in (CQ, FQ, FK, FV):
            send_x(a)
        wait_bytes(kv.at[OWN], own_in.at[0])
        for c in range(direct):
            pass_out(kv.at[OWN, :, :, cols(c)], END, c)
        pass_across(0)
        wait_text()
        wait_bytes(fx.at[CQ], x_in.at[0])
        half = heads // 2
        cross_heads(0, half)
        if direct:
            wait_bytes(kv.at[ACROSS, :, :, early], across_in.at[0])
        for c in range(direct):
            pass_out(kv.at[ACROSS, :, :, cols(c)], ACROSS, c)
        if nch > 1:
            pass_across(1)
        cross_heads(half, heads)
        send_cross()
        for c in range(2, nch):
            pass_across(c)
        wait_bytes(fx.at[FQ], x_in.at[1])
        wait_bytes(fx.at[pl.ds(FK, 2)], x_in.at[2])
        wait_bytes(kv.at[ACROSS, :, :, late], across_in.at[1])
        for c in range(direct):
            far = kv.at[FAR, :, :, cols(c)]
            wait_bytes(far, far_in.at[c])
            pass_out(far, FAR, c)
            attend_own(c)
            send_out(outs, so, cols(c), sent.at[5], out_in.at[0])
        wait_bytes(dq.at[:, late], q_in.at[0])
        wait_bytes(part.at[:, late], part_in.at[0])
        wait_bytes(stat.at[0], part_in.at[1])
        for c in range(direct, nch):
            wait_bytes(kv.at[FAR, :, :, cols(c)], far_in.at[c])
            attend_end(c)
            for k in range(n_head - 1, -1, -1):
                to = lax.rem(h + k, n_head)
                remote(
                    rows_of(oute, to, cols(c)), out_at(so, cols(c)),
                    sent.at[4], out_in.at[0], patch=outer, head=to,
                ).start()
            attend_own(c)
            send_out(outs, so, cols(c), sent.at[5], out_in.at[0])
        wait_bytes(kv.at[ACROSS], sent.at[2])
        wait_bytes(kv.at[FAR], sent.at[3])
        wait_bytes(oute.at[:, late], sent.at[4])
        wait_peers(outs, slice(0, hcols), sent.at[5])
        if direct:
            wait_bytes(kv.at[pl.ds(END, 3), :, :, early], sent.at[6])

    pl.when(is_end)(end_program)
    pl.when(jnp.logical_not(is_end))(middle_program)
    if n_head > 1:
        wait_bytes(fx.at[:, pl.ds(0, rows * (n_head - 1)), :], sent.at[0])
    wait_peers(outc, slice(0, hcols), sent.at[1])
    wait_bytes(co, out_in.at[1])
    wait_bytes(so, out_in.at[0])


def quad_attention(n_head, *args):
    fq, fk, fv, sk, sv, cq, tk, tv, mask = args
    prows = fq.shape[1] * n_head
    hcols = sk.shape[2]
    heads = hcols // HD
    nch = len(chunk_sizes(heads))
    direct = min(DIRECT, nch - 1)
    txt = tk.shape[1]
    dma = pltpu.SemaphoreType.DMA
    bf16 = jnp.bfloat16
    patch = pltpu.VMEM((prows, hcols), bf16)
    return pl.pallas_call(
        functools.partial(quad_kernel, n_head, direct),
        out_shape=(pltpu.VMEM(fq.shape, bf16), pltpu.VMEM(cq.shape, bf16)),
        in_specs=[pl.BlockSpec(memory_space=pl.ANY)] * 9,
        out_specs=(pl.BlockSpec(memory_space=pltpu.VMEM),) * 2,
        scratch_shapes=[
            pltpu.VMEM((4, prows, hcols), bf16),
            pltpu.VMEM((4, 2, prows, hcols), bf16),
            pltpu.VMEM((2, txt, hcols), bf16),
            pltpu.VMEM((1, txt), jnp.int32),
            patch,
            patch,
            pltpu.VMEM((2, prows, HD), jnp.float32),
            patch,
            patch,
            patch,
            dma((3,)),
            dma((2,)),
            dma((1,)),
            dma((nch,)),
            dma((nch,)),
            dma((2,)),
            dma((1,)),
            dma((2,)),
            dma((2,)),
            dma((7,)),
        ],
        compiler_params=pltpu.CompilerParams(collective_id=0, has_side_effects=True),
        name="displaced_attention",
    )(*args)


def store_kernel(a, b, so, co, sem):
    copies = [
        pltpu.make_async_copy(a, so, sem.at[0]),
        pltpu.make_async_copy(b, co, sem.at[1]),
    ]
    for cp in copies:
        cp.start()
    for cp in copies:
        cp.wait()


def store(a, b):
    return pl.pallas_call(
        store_kernel,
        out_shape=(
            jax.ShapeDtypeStruct(a.shape, a.dtype),
            jax.ShapeDtypeStruct(b.shape, b.dtype),
        ),
        in_specs=[pl.BlockSpec(memory_space=pltpu.VMEM)] * 2,
        out_specs=(pl.BlockSpec(memory_space=pltpu.HBM),) * 2,
        scratch_shapes=[pltpu.SemaphoreType.DMA((2,))],
        compiler_params=pltpu.CompilerParams(vmem_limit_bytes=1024 * 1024),
        name="store_outputs",
    )(a, b)


def per_device(n_patch, n_head, *args):
    if n_patch == 4:
        return store(*quad_attention(n_head, *args))
    return store(*line_attention(n_patch, n_head, *args))


def solution(mesh):
    return jax.shard_map(
        functools.partial(per_device, mesh.shape["patch"], mesh.shape["head"]),
        mesh=mesh,
        in_specs=(
            P(("group", "cfg"), ("patch", "head"), None),
            P(("group", "cfg"), ("patch", "head"), None),
            P(("group", "cfg"), ("patch", "head"), None),
            P(("group", "cfg"), "patch", "head"),
            P(("group", "cfg"), "patch", "head"),
            P(("group", "cfg"), ("patch", "head"), None),
            P(("group", "cfg"), None, "head"),
            P(("group", "cfg"), None, "head"),
            P(("group", "cfg"), None),
        ),
        out_specs=(
            P(("group", "cfg"), ("patch", "head"), None),
            P(("group", "cfg"), ("patch", "head"), None),
        ),
        check_vma=False,
    )
```

```python
import functools
import math

import jax
import jax.numpy as jnp
from jax import lax
from jax.experimental import pallas as pl
from jax.experimental.pallas import tpu as pltpu
from jax.sharding import PartitionSpec as P

HD = 128
MESH = pl.DeviceIdType.MESH


def dot_nt(a, b):
    return lax.dot_general(a, b, (((1,), (1,)), ((), ())), preferred_element_type=jnp.float32)


def line_kernel(
    n_patch, n_head, nch,
    fq, fk, fv, sk, sv, cq, tk, tv, mask,
    so, co,
    fx, kv, txk, txv, mk, outs, outc,
    x_send, x_recv, x_loc, t_loc, kv_loc, own_send, fwd_send, kv_recv,
    o_send, o_recv, o_loc, c_send, c_recv, c_loc,
):
    p = lax.axis_index("patch")
    h = lax.axis_index("head")
    rows = fq.shape[1]
    prows = rows * n_head
    hcols = sk.shape[2]
    ccols = hcols // nch
    heads = hcols // HD
    cheads = heads // nch
    scale = 1.0 / math.sqrt(HD)
    fresh = (cq, fq, fk, fv)
    my_rows = pl.ds(pl.multiple_of(h * rows, rows), rows)

    for c in range(nch):
        for i, ref in enumerate((sk, sv)):
            pltpu.make_async_copy(
                ref.at[0, :, pl.ds(c * ccols, ccols)], kv.at[p, c, i], kv_loc.at[c, i]
            ).start()
    text_copies = [
        pltpu.make_async_copy(mask, mk, t_loc.at[0]),
        pltpu.make_async_copy(tk.at[0], txk, t_loc.at[1]),
        pltpu.make_async_copy(tv.at[0], txv, t_loc.at[2]),
    ]
    own_copies = [
        pltpu.make_async_copy(
            ref.at[0, :, pl.ds(pl.multiple_of(h * hcols, hcols), hcols)],
            fx.at[a, my_rows, :],
            x_loc.at[a],
        )
        for a, ref in enumerate(fresh)
    ]
    for cp in own_copies + text_copies:
        cp.start()

    barrier = pltpu.get_barrier_semaphore()
    has_right = p < n_patch - 1
    has_left = p > 0

    @pl.when(has_right)
    def _():
        pl.semaphore_signal(barrier, inc=1, device_id={"patch": p + 1}, device_id_type=MESH)

    @pl.when(has_left)
    def _():
        pl.semaphore_signal(barrier, inc=1, device_id={"patch": p - 1}, device_id_type=MESH)

    for k in range(1, n_head):
        pl.semaphore_signal(
            barrier, inc=1, device_id={"head": lax.rem(h + k, n_head)}, device_id_type=MESH
        )
    pl.semaphore_wait(
        barrier, n_head - 1 + has_right.astype(jnp.int32) + has_left.astype(jnp.int32)
    )

    def x_copy(a, k):
        peer = lax.rem(h + k, n_head)
        return pltpu.make_async_remote_copy(
            src_ref=fresh[a].at[0, :, pl.ds(pl.multiple_of(peer * hcols, hcols), hcols)],
            dst_ref=fx.at[a, my_rows, :],
            send_sem=x_send.at[a, k - 1],
            recv_sem=x_recv.at[a, k - 1],
            device_id={"head": peer},
            device_id_type=MESH,
        )

    def kv_copy(src, c, target, sem):
        return pltpu.make_async_remote_copy(
            src_ref=kv.at[src, c],
            dst_ref=kv.at[src, c],
            send_sem=sem,
            recv_sem=kv_recv.at[src, c],
            device_id={"patch": target},
            device_id_type=MESH,
        )

    def start_x():
        for a in (1, 0, 2, 3):
            for k in range(1, n_head):
                x_copy(a, k).start()

    def wait_own_kv(c):
        for i, ref in enumerate((sk, sv)):
            pltpu.make_async_copy(
                ref.at[0, :, pl.ds(c * ccols, ccols)], kv.at[p, c, i], kv_loc.at[c, i]
            ).wait()

    def wait_x(a):
        own_copies[a].wait()
        for k in range(1, n_head):
            x_copy(a, k).wait_recv()

    def out_copy(src, dst, c, k, send, recv):
        peer = lax.rem(h + k, n_head)
        return pltpu.make_async_remote_copy(
            src_ref=src.at[c, pl.ds(pl.multiple_of(peer * rows, rows), rows), :],
            dst_ref=dst.at[0, :, pl.ds(pl.multiple_of(h * hcols + c * ccols, HD), ccols)],
            send_sem=send.at[c, k - 1],
            recv_sem=recv.at[c, k - 1],
            device_id={"head": peer},
            device_id_type=MESH,
        )

    def local_out(src, dst, c, sem):
        return pltpu.make_async_copy(
            src.at[c, my_rows, :],
            dst.at[0, :, pl.ds(pl.multiple_of(h * hcols + c * ccols, HD), ccols)],
            sem.at[c],
        )

    def send_out(src, dst, c, send, recv, loc):
        for k in range(1, n_head):
            out_copy(src, dst, c, k, send, recv).start()
        local_out(src, dst, c, loc).start()

    def cross_chunk(c):
        usable = mk[...] > 0
        for i in range(cheads):
            cols = pl.ds((c * cheads + i) * HD, HD)
            scores = dot_nt(fx[0, :, cols], txk[:, cols]) * scale
            scores = jnp.where(usable, scores, -jnp.inf)
            top = jnp.max(scores, axis=-1, keepdims=True)
            weights = jnp.exp(scores - top)
            total = jnp.sum(weights, axis=-1, keepdims=True)
            mix = jnp.dot(
                weights.astype(jnp.bfloat16), txv[:, cols], preferred_element_type=jnp.float32
            )
            outc[c, :, i * HD : (i + 1) * HD] = (mix / total).astype(jnp.bfloat16)

    def query(j):
        return fx[1, :, pl.ds(j * HD, HD)]

    def weigh(q, keys, values, top=None):
        scores = dot_nt(q, keys) * scale
        new_top = jnp.max(scores, axis=-1, keepdims=True)
        if top is not None:
            new_top = jnp.maximum(top, new_top)
        weights = jnp.exp(scores - new_top).astype(jnp.bfloat16)
        wide = jnp.concatenate([values, jnp.ones_like(values)], axis=1)
        mixed = jnp.dot(weights, wide, preferred_element_type=jnp.float32)
        return new_top, mixed[:, HD:], mixed[:, :HD]

    def absorb_rows(state, q, keys, values):
        top, total, mix = state
        new_top, more_total, more_mix = weigh(q, keys, values, top)
        factor = jnp.exp(top - new_top)
        return new_top, total * factor + more_total, mix * factor + more_mix

    def kv_rows(i, j, *sources):
        c, k = divmod(j, cheads)
        parts = [kv[src, c, i, :, pl.ds(k * HD, HD)] for src in sources]
        return parts[0] if len(parts) == 1 else jnp.concatenate(parts, axis=0)

    def fresh_rows(i, j):
        return fx[2 + i, :, pl.ds(j * HD, HD)]

    def first(j):
        return weigh(query(j), fresh_rows(0, j), fresh_rows(1, j))

    def absorb(state, src, j):
        return absorb_rows(state, query(j), kv_rows(0, j, src), kv_rows(1, j, src))

    def line_program():
        start_x()
        for c in range(nch):
            wait_own_kv(c)

            @pl.when(has_right)
            def _():
                kv_copy(p, c, p + 1, own_send.at[0, c]).start()

            @pl.when(has_left)
            def _():
                kv_copy(p, c, p - 1, own_send.at[1, c]).start()

        shorter = jnp.minimum(p, n_patch - 1 - p)

        def slot_source(s):
            near = s // 2 + 1
            near_src = jnp.where(s % 2 == 0, p - near, p + near)
            far = s - shorter + 1
            far_src = jnp.where(p > shorter, p - far, p + far)
            return jnp.where(s < 2 * shorter, near_src, far_src)

        def forward_target(src):
            target = jnp.where(src < p, p + 1, p - 1)
            return target, (target >= 0) & (target < n_patch)

        def forward(s, c):
            src = slot_source(s)
            kv_copy(src, c, p, fwd_send.at[s, c]).wait_recv()
            target, valid = forward_target(src)

            @pl.when(valid)
            def _():
                kv_copy(src, c, target, fwd_send.at[s, c]).start()

        half = (nch + 1) // 2
        for cp in text_copies:
            cp.wait()
        wait_x(0)
        for c in range(half):
            cross_chunk(c)
        for c in range(half):
            forward(0, c)
        for c in range(half, nch):
            cross_chunk(c)
        for c in range(nch):
            send_out(outc, co, c, c_send, c_recv, c_loc)
        for c in range(half, nch):
            forward(0, c)
        for a in range(1, 4):
            wait_x(a)
        states = [first(j) for j in range(heads)]
        src = slot_source(0)
        states = [absorb(states[j], src, j) for j in range(heads)]

        def slot(s, states):
            src = slot_source(s)
            out = []
            for c in range(nch):
                forward(s, c)
                for j in range(c * cheads, (c + 1) * cheads):
                    out.append(absorb(states[j], src, j))
            return out

        if n_patch <= 8:
            for s in range(1, n_patch - 2):
                states = slot(s, states)
        else:
            states = lax.fori_loop(1, n_patch - 2, slot, states)
        last = n_patch - 2
        src = slot_source(last)
        for c in range(nch):
            if last > 0:
                forward(last, c)
            for i in range(cheads):
                j = c * cheads + i
                _, total, mix = absorb(states[j], src, j) if last > 0 else states[j]
                outs[c, :, i * HD : (i + 1) * HD] = (mix / total).astype(jnp.bfloat16)
            if c > 0:
                send_out(outs, so, c - 1, o_send, o_recv, o_loc)
        send_out(outs, so, nch - 1, o_send, o_recv, o_loc)

        for c in range(nch):

            @pl.when(has_right)
            def _():
                kv_copy(p, c, p + 1, own_send.at[0, c]).wait_send()

            @pl.when(has_left)
            def _():
                kv_copy(p, c, p - 1, own_send.at[1, c]).wait_send()

        def drain(s, carry):
            for c in range(nch):
                target, valid = forward_target(slot_source(s))

                @pl.when(valid)
                def _():
                    kv_copy(slot_source(s), c, target, fwd_send.at[s, c]).wait_send()

            return carry

        if n_patch <= 8:
            for s in range(n_patch - 1):
                drain(s, 0)
        else:
            lax.fori_loop(0, n_patch - 1, drain, 0)

    line_program()

    for a in range(4):
        for k in range(1, n_head):
            x_copy(a, k).wait_send()
    for src_ref, dst, send, recv, loc in (
        (outc, co, c_send, c_recv, c_loc),
        (outs, so, o_send, o_recv, o_loc),
    ):
        for c in range(nch):
            for k in range(1, n_head):
                cp = out_copy(src_ref, dst, c, k, send, recv)
                cp.wait_send()
                cp.wait_recv()
            local_out(src_ref, dst, c, loc).wait()


def line_attention(n_patch, n_head, *args):
    fq, fk, fv, sk, sv, cq, tk, tv, mask = args
    rows = fq.shape[1]
    prows = rows * n_head
    hcols = sk.shape[2]
    heads = hcols // HD
    nch = 2 if heads % 2 == 0 else 1
    ccols = hcols // nch
    txt = tk.shape[1]
    peers = max(n_head - 1, 1)
    any_spec = pl.BlockSpec(memory_space=pl.ANY)
    dma = pltpu.SemaphoreType.DMA
    bf16 = jnp.bfloat16
    mixed = pl.pallas_call(
        functools.partial(line_kernel, n_patch, n_head, nch),
        out_shape=(
            pltpu.VMEM(fq.shape, bf16),
            pltpu.VMEM(cq.shape, bf16),
        ),
        in_specs=[any_spec] * 9,
        out_specs=(pl.BlockSpec(memory_space=pltpu.VMEM),) * 2,
        scratch_shapes=[
            pltpu.VMEM((4, prows, hcols), bf16),
            pltpu.VMEM((n_patch, nch, 2, prows, ccols), bf16),
            pltpu.VMEM((txt, hcols), bf16),
            pltpu.VMEM((txt, hcols), bf16),
            pltpu.VMEM((1, txt), jnp.int32),
            pltpu.VMEM((nch, prows, ccols), bf16),
            pltpu.VMEM((nch, prows, ccols), bf16),
            dma((4, peers)),
            dma((4, peers)),
            dma((4,)),
            dma((3,)),
            dma((nch, 2)),
            dma((2, nch)),
            dma((n_patch, nch)),
            dma((n_patch, nch)),
            dma((nch, peers)),
            dma((nch, peers)),
            dma((nch,)),
            dma((nch, peers)),
            dma((nch, peers)),
            dma((nch,)),
        ],
        compiler_params=pltpu.CompilerParams(collective_id=0, has_side_effects=True),
        name="displaced_attention",
    )(*args)
    return mixed


END, ACROSS, FAR, OWN = range(4)
CQ, FQ, FK, FV = range(4)
DIRECT = 2
CROSS = 2


def chunk_heads(heads):
    return max(n for n in range(1, max(1, heads // 5) + 1) if heads % n == 0)


def quad_kernel(
    n_head, direct,
    fq, fk, fv, sk, sv, cq, tk, tv, mask,
    so, co,
    fx, kv, tx, mk, dq, part, stat, spread, outs, oute, outc,
    x_in, t_in, own_in, end_in, far_in, across_in, q_in, part_in, out_in, sent,
):
    p = lax.axis_index("patch")
    h = lax.axis_index("head")
    rows = fq.shape[1]
    prows = rows * n_head
    hcols = sk.shape[2]
    heads = hcols // HD
    cheads = chunk_heads(heads)
    nch = heads // cheads
    size = cheads * HD
    early = pl.ds(0, direct * size)
    late = pl.ds(direct * size, hcols - direct * size)
    every = pl.ds(0, hcols)
    scale = 1.0 / math.sqrt(HD)
    fresh = (cq, fq, fk, fv)
    x_sem = (0, 1, 2, 2)
    across = 3 - p
    is_end = (p == 0) | (p == 3)
    inner = jnp.where(p < 2, 1, 2)
    outer = jnp.where(p < 2, 0, 3)
    my_rows = pl.ds(pl.multiple_of(h * rows, rows), rows)

    def head_cols(who):
        return pl.ds(pl.multiple_of(who * hcols, hcols), hcols)

    def cols(c):
        return pl.ds(c * size if isinstance(c, int) else pl.multiple_of(c * size, size), size)

    def head_at(j):
        return pl.ds(j * HD if isinstance(j, int) else pl.multiple_of(j * HD, HD), HD)

    def own_copy(a):
        return pltpu.make_async_copy(
            fresh[a].at[0, :, head_cols(h)], fx.at[a, my_rows, :], x_in.at[x_sem[a]]
        )

    def remote(src, dst, send, recv, **to):
        return pltpu.make_async_remote_copy(
            src_ref=src, dst_ref=dst, send_sem=send, recv_sem=recv,
            device_id=to, device_id_type=MESH,
        )

    def wait_bytes(ref, sem):
        pltpu.make_async_copy(ref, ref, sem).wait()

    def load_text():
        pltpu.make_async_copy(mask, mk, t_in.at[0]).start()
        pltpu.make_async_copy(tk.at[0], tx.at[0], t_in.at[1]).start()
        pltpu.make_async_copy(tv.at[0], tx.at[1], t_in.at[1]).start()

    barrier = pltpu.get_barrier_semaphore()
    for k in range(1, n_head):
        pl.semaphore_signal(
            barrier, inc=1, device_id={"head": lax.rem(h + k, n_head)}, device_id_type=MESH
        )

    @pl.when(is_end)
    def _():
        pl.semaphore_signal(barrier, inc=1, device_id={"patch": inner}, device_id_type=MESH)

    @pl.when(jnp.logical_not(is_end))
    def _():
        pl.semaphore_signal(barrier, inc=1, device_id={"patch": across}, device_id_type=MESH)
        pl.semaphore_signal(barrier, inc=1, device_id={"patch": outer}, device_id_type=MESH)
        for i, ref in enumerate((sk, sv)):
            pltpu.make_async_copy(ref.at[0], kv.at[OWN, i], own_in.at[0]).start()

    for a in range(4):
        own_copy(a).start()
    load_text()
    pl.semaphore_wait(barrier, n_head - 1 + jnp.where(is_end, 1, 2))

    def send_x(a):
        for k in range(1, n_head):
            peer = lax.rem(h + k, n_head)
            remote(
                fresh[a].at[0, :, head_cols(peer)], fx.at[a, my_rows, :],
                sent.at[0], x_in.at[x_sem[a]], head=peer,
            ).start()

    def scores_of(q, keys):
        return dot_nt(q, keys) * scale

    def mix_of(weights, values):
        wide = jnp.concatenate([values, jnp.ones_like(values)], axis=1)
        mixed = jnp.dot(
            weights.astype(jnp.bfloat16), wide, preferred_element_type=jnp.float32
        )
        return mixed[:, :HD], mixed[:, HD:]

    def own_head(at):
        keys, values = (
            jnp.concatenate([fx[FK + i, :, at]] + [kv[s, i, :, at] for s in (END, ACROSS, FAR)])
            for i in range(2)
        )
        scores = scores_of(fx[FQ, :, at], keys)
        mix, total = mix_of(jnp.exp(scores - jnp.max(scores, axis=-1, keepdims=True)), values)
        return (mix / total).astype(jnp.bfloat16)

    def end_head(at, lse):
        keys, values = (
            jnp.concatenate([kv[s, i, :, at] for s in (OWN, ACROSS, FAR)]) for i in range(2)
        )
        scores = scores_of(dq[:, at], keys)
        top = jnp.maximum(jnp.max(scores, axis=-1, keepdims=True), lse)
        mix, total = mix_of(jnp.exp(scores - top[:, :1]), values)
        theirs = jnp.exp(lse - top)
        mix = mix + part[:, at].astype(jnp.float32) * theirs
        return (mix / (total + theirs)).astype(jnp.bfloat16)

    def attend(c, both):
        results = []
        for i in range(cheads):
            j = c * cheads + i
            at = head_at(j)
            if both:
                results.append((oute, at, end_head(at, spread[j])))
            results.append((outs, at, own_head(at)))
        for ref, at, value in results:
            ref[:, at] = value

    def cross_heads(first, last):
        usable = mk[...] > 0

        def one(j):
            at = head_at(j)
            scores = jnp.where(usable, scores_of(fx[CQ, :, at], tx[0, :, at]), -jnp.inf)
            weights = jnp.exp(scores - jnp.max(scores, axis=-1, keepdims=True))
            total = jnp.sum(weights, axis=-1, keepdims=True)
            mix = jnp.dot(
                weights.astype(jnp.bfloat16), tx[1, :, at], preferred_element_type=jnp.float32
            )
            return at, (mix / total).astype(jnp.bfloat16)

        def step(s, carry):
            done = [one(first + s * CROSS + i) for i in range(CROSS)]
            for at, value in done:
                outc[:, at] = value
            return carry

        lax.fori_loop(0, (last - first) // CROSS, step, 0)
        for j in range(last - (last - first) % CROSS, last):
            at, value = one(j)
            outc[:, at] = value

    def out_at(dst, at):
        return dst.at[0, :, pl.ds(pl.multiple_of(h * hcols + at.start, HD), at.size)]

    def rows_of(src, who, at):
        return src.at[pl.ds(pl.multiple_of(who * rows, rows), rows), at]

    def send_out(src, dst, at, send, recv):
        for k in range(1, n_head):
            peer = lax.rem(h + k, n_head)
            remote(rows_of(src, peer, at), out_at(dst, at), send, recv, head=peer).start()
        pltpu.make_async_copy(rows_of(src, h, at), out_at(dst, at), recv).start()

    def wait_peers(src, at, send):
        if n_head > 1:
            wait_bytes(src.at[pl.ds(0, rows * (n_head - 1)), at], send)

    def send_cross():
        send_out(outc, co, every, sent.at[1], out_in.at[1])

    def wait_text():
        wait_bytes(mk, t_in.at[0])
        wait_bytes(tx, t_in.at[1])

    def end_program():
        def send_kv(c):
            for i, ref in enumerate((sk, sv)):
                remote(
                    ref.at[0, :, cols(c)], kv.at[END, i, :, cols(c)],
                    sent.at[2], end_in.at[c], patch=inner,
                ).start()

        lead = (nch + 1) // 2
        send_x(FQ)
        send_kv(0)
        send_x(FK)
        send_x(FV)
        send_x(CQ)
        for c in range(1, lead):
            send_kv(c)
        wait_bytes(fx.at[FQ], x_in.at[1])
        remote(
            fx.at[FQ, :, late], dq.at[:, late], sent.at[3], q_in.at[0], patch=inner
        ).start()
        for c in range(lead, nch):
            send_kv(c)
        wait_bytes(fx.at[pl.ds(FK, 2)], x_in.at[2])
        lanes = lax.broadcasted_iota(jnp.int32, (prows, HD), 1)
        lse = jnp.zeros((prows, HD), jnp.float32)
        for j in range(direct * cheads, heads):
            at = slice(j * HD, (j + 1) * HD)
            scores = scores_of(fx[FQ, :, at], fx[FK, :, at])
            top = jnp.max(scores, axis=-1, keepdims=True)
            mix, total = mix_of(jnp.exp(scores - top), fx[FV, :, at])
            outs[:, at] = (mix / total).astype(jnp.bfloat16)
            lse = jnp.where(lanes == j, top + jnp.log(total), lse)
        stat[1] = lse
        remote(
            outs.at[:, late], part.at[:, late], sent.at[4], part_in.at[0], patch=inner
        ).start()
        remote(stat.at[1], stat.at[0], sent.at[5], part_in.at[1], patch=inner).start()
        wait_text()
        wait_bytes(fx.at[CQ], x_in.at[0])
        cross_heads(0, heads)
        send_cross()

        def direct_chunk(c, carry):
            wait_bytes(kv.at[pl.ds(END, 3), :, :, cols(c)], far_in.at[c])
            attend(c, False)
            send_out(outs, so, cols(c), sent.at[6], out_in.at[0])
            return carry

        if direct:
            lax.fori_loop(0, direct, direct_chunk, 0)
        wait_bytes(kv.at[END], sent.at[2])
        wait_bytes(dq.at[:, late], sent.at[3])
        wait_bytes(part.at[:, late], sent.at[4])
        wait_bytes(stat.at[0], sent.at[5])
        if direct:
            wait_peers(outs, early, sent.at[6])

    def middle_program():
        def send_own(at, recv):
            for i, ref in enumerate((sk, sv)):
                remote(
                    ref.at[0, :, at], kv.at[ACROSS, i, :, at], sent.at[2], recv, patch=across
                ).start()

        def pass_out(src, slot, c):
            remote(
                src, kv.at[slot, :, :, cols(c)], sent.at[6], far_in.at[c], patch=outer
            ).start()

        def pass_across(c):
            src = kv.at[END, :, :, cols(c)]
            wait_bytes(src, end_in.at[c])
            remote(
                src, kv.at[FAR, :, :, cols(c)], sent.at[3], far_in.at[c], patch=across
            ).start()

        if direct:
            send_own(early, across_in.at[0])
        send_own(late, across_in.at[1])
        for a in (CQ, FQ, FK, FV):
            send_x(a)
        wait_bytes(kv.at[OWN], own_in.at[0])
        for c in range(direct):
            pass_out(kv.at[OWN, :, :, cols(c)], END, c)
        pass_across(0)
        wait_text()
        wait_bytes(fx.at[CQ], x_in.at[0])
        half = heads // 2
        cross_heads(0, half)
        if direct:
            wait_bytes(kv.at[ACROSS, :, :, early], across_in.at[0])
        for c in range(direct):
            pass_out(kv.at[ACROSS, :, :, cols(c)], ACROSS, c)
        if nch > 1:
            pass_across(1)
        cross_heads(half, heads)
        send_cross()
        for c in range(2, nch):
            pass_across(c)
        wait_bytes(fx.at[FQ], x_in.at[1])
        wait_bytes(fx.at[pl.ds(FK, 2)], x_in.at[2])
        wait_bytes(kv.at[ACROSS, :, :, late], across_in.at[1])
        def own_chunk(c, carry):
            far = kv.at[FAR, :, :, cols(c)]
            wait_bytes(far, far_in.at[c])
            pass_out(far, FAR, c)
            attend(c, False)
            send_out(outs, so, cols(c), sent.at[5], out_in.at[0])
            return carry

        def both_chunk(c, carry):
            wait_bytes(kv.at[FAR, :, :, cols(c)], far_in.at[c])
            attend(c, True)
            for k in range(n_head - 1, -1, -1):
                to = lax.rem(h + k, n_head)
                remote(
                    rows_of(oute, to, cols(c)), out_at(so, cols(c)),
                    sent.at[4], out_in.at[0], patch=outer, head=to,
                ).start()
            send_out(outs, so, cols(c), sent.at[5], out_in.at[0])
            return carry

        if direct:
            lax.fori_loop(0, direct, own_chunk, 0)
        wait_bytes(stat.at[0], part_in.at[1])
        for j in range(direct * cheads, heads):
            spread[j] = jnp.broadcast_to(stat[0, :, j : j + 1], (prows, HD))
        wait_bytes(dq.at[:, late], q_in.at[0])
        wait_bytes(part.at[:, late], part_in.at[0])
        lax.fori_loop(direct, nch, both_chunk, 0)
        wait_bytes(kv.at[ACROSS], sent.at[2])
        wait_bytes(kv.at[FAR], sent.at[3])
        wait_bytes(oute.at[:, late], sent.at[4])
        wait_peers(outs, every, sent.at[5])
        if direct:
            wait_bytes(kv.at[pl.ds(END, 3), :, :, early], sent.at[6])

    pl.when(is_end)(end_program)
    pl.when(jnp.logical_not(is_end))(middle_program)
    if n_head > 1:
        wait_bytes(fx.at[:, pl.ds(0, rows * (n_head - 1)), :], sent.at[0])
    wait_peers(outc, every, sent.at[1])
    wait_bytes(co, out_in.at[1])
    wait_bytes(so, out_in.at[0])


def quad_attention(n_head, *args):
    fq, fk, fv, sk, sv, cq, tk, tv, mask = args
    prows = fq.shape[1] * n_head
    hcols = sk.shape[2]
    heads = hcols // HD
    nch = heads // chunk_heads(heads)
    direct = min(DIRECT, nch - 1)
    txt = tk.shape[1]
    dma = pltpu.SemaphoreType.DMA
    bf16 = jnp.bfloat16
    patch = pltpu.VMEM((prows, hcols), bf16)
    return pl.pallas_call(
        functools.partial(quad_kernel, n_head, direct),
        out_shape=(pltpu.VMEM(fq.shape, bf16), pltpu.VMEM(cq.shape, bf16)),
        in_specs=[pl.BlockSpec(memory_space=pl.ANY)] * 9,
        out_specs=(pl.BlockSpec(memory_space=pltpu.VMEM),) * 2,
        scratch_shapes=[
            pltpu.VMEM((4, prows, hcols), bf16),
            pltpu.VMEM((4, 2, prows, hcols), bf16),
            pltpu.VMEM((2, txt, hcols), bf16),
            pltpu.VMEM((1, txt), jnp.int32),
            patch,
            patch,
            pltpu.VMEM((2, prows, HD), jnp.float32),
            pltpu.VMEM((heads, prows, HD), jnp.float32),
            patch,
            patch,
            patch,
            dma((3,)),
            dma((2,)),
            dma((1,)),
            dma((nch,)),
            dma((nch,)),
            dma((2,)),
            dma((1,)),
            dma((2,)),
            dma((2,)),
            dma((7,)),
        ],
        compiler_params=pltpu.CompilerParams(collective_id=0, has_side_effects=True),
        name="displaced_attention",
    )(*args)


def store_kernel(a, b, so, co, sem):
    copies = [
        pltpu.make_async_copy(a, so, sem.at[0]),
        pltpu.make_async_copy(b, co, sem.at[1]),
    ]
    for cp in copies:
        cp.start()
    for cp in copies:
        cp.wait()


def store(a, b):
    return pl.pallas_call(
        store_kernel,
        out_shape=(
            jax.ShapeDtypeStruct(a.shape, a.dtype),
            jax.ShapeDtypeStruct(b.shape, b.dtype),
        ),
        in_specs=[pl.BlockSpec(memory_space=pltpu.VMEM)] * 2,
        out_specs=(pl.BlockSpec(memory_space=pltpu.HBM),) * 2,
        scratch_shapes=[pltpu.SemaphoreType.DMA((2,))],
        compiler_params=pltpu.CompilerParams(vmem_limit_bytes=1024 * 1024),
        name="store_outputs",
    )(a, b)


def per_device(n_patch, n_head, *args):
    if n_patch == 4:
        return store(*quad_attention(n_head, *args))
    return store(*line_attention(n_patch, n_head, *args))


def solution(mesh):
    return jax.shard_map(
        functools.partial(per_device, mesh.shape["patch"], mesh.shape["head"]),
        mesh=mesh,
        in_specs=(
            P(("group", "cfg"), ("patch", "head"), None),
            P(("group", "cfg"), ("patch", "head"), None),
            P(("group", "cfg"), ("patch", "head"), None),
            P(("group", "cfg"), "patch", "head"),
            P(("group", "cfg"), "patch", "head"),
            P(("group", "cfg"), ("patch", "head"), None),
            P(("group", "cfg"), None, "head"),
            P(("group", "cfg"), None, "head"),
            P(("group", "cfg"), None),
        ),
        out_specs=(
            P(("group", "cfg"), ("patch", "head"), None),
            P(("group", "cfg"), ("patch", "head"), None),
        ),
        check_vma=False,
    )
```

```python
import functools
import math

import jax
import jax.numpy as jnp
from jax import lax
from jax.experimental import pallas as pl
from jax.experimental.pallas import tpu as pltpu
from jax.sharding import PartitionSpec as P

HD = 128
MESH = pl.DeviceIdType.MESH


def dot_nt(a, b):
    return lax.dot_general(a, b, (((1,), (1,)), ((), ())), preferred_element_type=jnp.float32)


def line_kernel(
    n_patch, n_head, nch,
    fq, fk, fv, sk, sv, cq, tk, tv, mask,
    so, co,
    fx, kv, txk, txv, mk, outs, outc,
    x_send, x_recv, x_loc, t_loc, kv_loc, own_send, fwd_send, kv_recv,
    o_send, o_recv, o_loc, c_send, c_recv, c_loc,
):
    p = lax.axis_index("patch")
    h = lax.axis_index("head")
    rows = fq.shape[1]
    prows = rows * n_head
    hcols = sk.shape[2]
    ccols = hcols // nch
    heads = hcols // HD
    cheads = heads // nch
    scale = 1.0 / math.sqrt(HD)
    fresh = (cq, fq, fk, fv)
    my_rows = pl.ds(pl.multiple_of(h * rows, rows), rows)

    for c in range(nch):
        for i, ref in enumerate((sk, sv)):
            pltpu.make_async_copy(
                ref.at[0, :, pl.ds(c * ccols, ccols)], kv.at[p, c, i], kv_loc.at[c, i]
            ).start()
    text_copies = [
        pltpu.make_async_copy(mask, mk, t_loc.at[0]),
        pltpu.make_async_copy(tk.at[0], txk, t_loc.at[1]),
        pltpu.make_async_copy(tv.at[0], txv, t_loc.at[2]),
    ]
    own_copies = [
        pltpu.make_async_copy(
            ref.at[0, :, pl.ds(pl.multiple_of(h * hcols, hcols), hcols)],
            fx.at[a, my_rows, :],
            x_loc.at[a],
        )
        for a, ref in enumerate(fresh)
    ]
    for cp in own_copies + text_copies:
        cp.start()

    barrier = pltpu.get_barrier_semaphore()
    has_right = p < n_patch - 1
    has_left = p > 0

    @pl.when(has_right)
    def _():
        pl.semaphore_signal(barrier, inc=1, device_id={"patch": p + 1}, device_id_type=MESH)

    @pl.when(has_left)
    def _():
        pl.semaphore_signal(barrier, inc=1, device_id={"patch": p - 1}, device_id_type=MESH)

    for k in range(1, n_head):
        pl.semaphore_signal(
            barrier, inc=1, device_id={"head": lax.rem(h + k, n_head)}, device_id_type=MESH
        )
    pl.semaphore_wait(
        barrier, n_head - 1 + has_right.astype(jnp.int32) + has_left.astype(jnp.int32)
    )

    def x_copy(a, k):
        peer = lax.rem(h + k, n_head)
        return pltpu.make_async_remote_copy(
            src_ref=fresh[a].at[0, :, pl.ds(pl.multiple_of(peer * hcols, hcols), hcols)],
            dst_ref=fx.at[a, my_rows, :],
            send_sem=x_send.at[a, k - 1],
            recv_sem=x_recv.at[a, k - 1],
            device_id={"head": peer},
            device_id_type=MESH,
        )

    def kv_copy(src, c, target, sem):
        return pltpu.make_async_remote_copy(
            src_ref=kv.at[src, c],
            dst_ref=kv.at[src, c],
            send_sem=sem,
            recv_sem=kv_recv.at[src, c],
            device_id={"patch": target},
            device_id_type=MESH,
        )

    def start_x():
        for a in (1, 0, 2, 3):
            for k in range(1, n_head):
                x_copy(a, k).start()

    def wait_own_kv(c):
        for i, ref in enumerate((sk, sv)):
            pltpu.make_async_copy(
                ref.at[0, :, pl.ds(c * ccols, ccols)], kv.at[p, c, i], kv_loc.at[c, i]
            ).wait()

    def wait_x(a):
        own_copies[a].wait()
        for k in range(1, n_head):
            x_copy(a, k).wait_recv()

    def out_copy(src, dst, c, k, send, recv):
        peer = lax.rem(h + k, n_head)
        return pltpu.make_async_remote_copy(
            src_ref=src.at[c, pl.ds(pl.multiple_of(peer * rows, rows), rows), :],
            dst_ref=dst.at[0, :, pl.ds(pl.multiple_of(h * hcols + c * ccols, HD), ccols)],
            send_sem=send.at[c, k - 1],
            recv_sem=recv.at[c, k - 1],
            device_id={"head": peer},
            device_id_type=MESH,
        )

    def local_out(src, dst, c, sem):
        return pltpu.make_async_copy(
            src.at[c, my_rows, :],
            dst.at[0, :, pl.ds(pl.multiple_of(h * hcols + c * ccols, HD), ccols)],
            sem.at[c],
        )

    def send_out(src, dst, c, send, recv, loc):
        for k in range(1, n_head):
            out_copy(src, dst, c, k, send, recv).start()
        local_out(src, dst, c, loc).start()

    def cross_chunk(c):
        usable = mk[...] > 0
        for i in range(cheads):
            cols = pl.ds((c * cheads + i) * HD, HD)
            scores = dot_nt(fx[0, :, cols], txk[:, cols]) * scale
            scores = jnp.where(usable, scores, -jnp.inf)
            top = jnp.max(scores, axis=-1, keepdims=True)
            weights = jnp.exp(scores - top)
            total = jnp.sum(weights, axis=-1, keepdims=True)
            mix = jnp.dot(
                weights.astype(jnp.bfloat16), txv[:, cols], preferred_element_type=jnp.float32
            )
            outc[c, :, i * HD : (i + 1) * HD] = (mix / total).astype(jnp.bfloat16)

    def query(j):
        return fx[1, :, pl.ds(j * HD, HD)]

    def weigh(q, keys, values, top=None):
        scores = dot_nt(q, keys) * scale
        new_top = jnp.max(scores, axis=-1, keepdims=True)
        if top is not None:
            new_top = jnp.maximum(top, new_top)
        weights = jnp.exp(scores - new_top).astype(jnp.bfloat16)
        wide = jnp.concatenate([values, jnp.ones_like(values)], axis=1)
        mixed = jnp.dot(weights, wide, preferred_element_type=jnp.float32)
        return new_top, mixed[:, HD:], mixed[:, :HD]

    def absorb_rows(state, q, keys, values):
        top, total, mix = state
        new_top, more_total, more_mix = weigh(q, keys, values, top)
        factor = jnp.exp(top - new_top)
        return new_top, total * factor + more_total, mix * factor + more_mix

    def kv_rows(i, j, *sources):
        c, k = divmod(j, cheads)
        parts = [kv[src, c, i, :, pl.ds(k * HD, HD)] for src in sources]
        return parts[0] if len(parts) == 1 else jnp.concatenate(parts, axis=0)

    def fresh_rows(i, j):
        return fx[2 + i, :, pl.ds(j * HD, HD)]

    def first(j):
        return weigh(query(j), fresh_rows(0, j), fresh_rows(1, j))

    def absorb(state, src, j):
        return absorb_rows(state, query(j), kv_rows(0, j, src), kv_rows(1, j, src))

    def line_program():
        start_x()
        for c in range(nch):
            wait_own_kv(c)

            @pl.when(has_right)
            def _():
                kv_copy(p, c, p + 1, own_send.at[0, c]).start()

            @pl.when(has_left)
            def _():
                kv_copy(p, c, p - 1, own_send.at[1, c]).start()

        shorter = jnp.minimum(p, n_patch - 1 - p)

        def slot_source(s):
            near = s // 2 + 1
            near_src = jnp.where(s % 2 == 0, p - near, p + near)
            far = s - shorter + 1
            far_src = jnp.where(p > shorter, p - far, p + far)
            return jnp.where(s < 2 * shorter, near_src, far_src)

        def forward_target(src):
            target = jnp.where(src < p, p + 1, p - 1)
            return target, (target >= 0) & (target < n_patch)

        def forward(s, c):
            src = slot_source(s)
            kv_copy(src, c, p, fwd_send.at[s, c]).wait_recv()
            target, valid = forward_target(src)

            @pl.when(valid)
            def _():
                kv_copy(src, c, target, fwd_send.at[s, c]).start()

        half = (nch + 1) // 2
        for cp in text_copies:
            cp.wait()
        wait_x(0)
        for c in range(half):
            cross_chunk(c)
        for c in range(half):
            forward(0, c)
        for c in range(half, nch):
            cross_chunk(c)
        for c in range(nch):
            send_out(outc, co, c, c_send, c_recv, c_loc)
        for c in range(half, nch):
            forward(0, c)
        for a in range(1, 4):
            wait_x(a)
        states = [first(j) for j in range(heads)]
        src = slot_source(0)
        states = [absorb(states[j], src, j) for j in range(heads)]

        def slot(s, states):
            src = slot_source(s)
            out = []
            for c in range(nch):
                forward(s, c)
                for j in range(c * cheads, (c + 1) * cheads):
                    out.append(absorb(states[j], src, j))
            return out

        if n_patch <= 8:
            for s in range(1, n_patch - 2):
                states = slot(s, states)
        else:
            states = lax.fori_loop(1, n_patch - 2, slot, states)
        last = n_patch - 2
        src = slot_source(last)
        for c in range(nch):
            if last > 0:
                forward(last, c)
            for i in range(cheads):
                j = c * cheads + i
                _, total, mix = absorb(states[j], src, j) if last > 0 else states[j]
                outs[c, :, i * HD : (i + 1) * HD] = (mix / total).astype(jnp.bfloat16)
            if c > 0:
                send_out(outs, so, c - 1, o_send, o_recv, o_loc)
        send_out(outs, so, nch - 1, o_send, o_recv, o_loc)

        for c in range(nch):

            @pl.when(has_right)
            def _():
                kv_copy(p, c, p + 1, own_send.at[0, c]).wait_send()

            @pl.when(has_left)
            def _():
                kv_copy(p, c, p - 1, own_send.at[1, c]).wait_send()

        def drain(s, carry):
            for c in range(nch):
                target, valid = forward_target(slot_source(s))

                @pl.when(valid)
                def _():
                    kv_copy(slot_source(s), c, target, fwd_send.at[s, c]).wait_send()

            return carry

        if n_patch <= 8:
            for s in range(n_patch - 1):
                drain(s, 0)
        else:
            lax.fori_loop(0, n_patch - 1, drain, 0)

    line_program()

    for a in range(4):
        for k in range(1, n_head):
            x_copy(a, k).wait_send()
    for src_ref, dst, send, recv, loc in (
        (outc, co, c_send, c_recv, c_loc),
        (outs, so, o_send, o_recv, o_loc),
    ):
        for c in range(nch):
            for k in range(1, n_head):
                cp = out_copy(src_ref, dst, c, k, send, recv)
                cp.wait_send()
                cp.wait_recv()
            local_out(src_ref, dst, c, loc).wait()


def line_attention(n_patch, n_head, *args):
    fq, fk, fv, sk, sv, cq, tk, tv, mask = args
    rows = fq.shape[1]
    prows = rows * n_head
    hcols = sk.shape[2]
    heads = hcols // HD
    nch = 2 if heads % 2 == 0 else 1
    ccols = hcols // nch
    txt = tk.shape[1]
    peers = max(n_head - 1, 1)
    any_spec = pl.BlockSpec(memory_space=pl.ANY)
    dma = pltpu.SemaphoreType.DMA
    bf16 = jnp.bfloat16
    mixed = pl.pallas_call(
        functools.partial(line_kernel, n_patch, n_head, nch),
        out_shape=(
            pltpu.VMEM(fq.shape, bf16),
            pltpu.VMEM(cq.shape, bf16),
        ),
        in_specs=[any_spec] * 9,
        out_specs=(pl.BlockSpec(memory_space=pltpu.VMEM),) * 2,
        scratch_shapes=[
            pltpu.VMEM((4, prows, hcols), bf16),
            pltpu.VMEM((n_patch, nch, 2, prows, ccols), bf16),
            pltpu.VMEM((txt, hcols), bf16),
            pltpu.VMEM((txt, hcols), bf16),
            pltpu.VMEM((1, txt), jnp.int32),
            pltpu.VMEM((nch, prows, ccols), bf16),
            pltpu.VMEM((nch, prows, ccols), bf16),
            dma((4, peers)),
            dma((4, peers)),
            dma((4,)),
            dma((3,)),
            dma((nch, 2)),
            dma((2, nch)),
            dma((n_patch, nch)),
            dma((n_patch, nch)),
            dma((nch, peers)),
            dma((nch, peers)),
            dma((nch,)),
            dma((nch, peers)),
            dma((nch, peers)),
            dma((nch,)),
        ],
        compiler_params=pltpu.CompilerParams(collective_id=0, has_side_effects=True),
        name="displaced_attention",
    )(*args)
    return mixed


END, ACROSS, FAR, OWN = range(4)
CQ, FQ, FK, FV = range(4)
DIRECT = 2
CROSS = 2


def chunk_heads(heads):
    return max(n for n in range(1, max(1, heads // 5) + 1) if heads % n == 0)


def quad_kernel(
    n_head, direct,
    fq, fk, fv, sk, sv, cq, tk, tv, mask,
    so, co,
    fx, kv, tx, mk, dq, part, stat, spread, outs, oute, outc,
    x_in, t_in, own_in, end_in, far_in, across_in, q_in, part_in, out_in, sent,
):
    p = lax.axis_index("patch")
    h = lax.axis_index("head")
    rows = fq.shape[1]
    prows = rows * n_head
    hcols = sk.shape[2]
    heads = hcols // HD
    cheads = chunk_heads(heads)
    nch = heads // cheads
    size = cheads * HD
    early = pl.ds(0, direct * size)
    late = pl.ds(direct * size, hcols - direct * size)
    every = pl.ds(0, hcols)
    scale = 1.0 / math.sqrt(HD)
    fresh = (cq, fq, fk, fv)
    x_sem = (0, 1, 2, 2)
    across = 3 - p
    is_end = (p == 0) | (p == 3)
    inner = jnp.where(p < 2, 1, 2)
    outer = jnp.where(p < 2, 0, 3)
    my_rows = pl.ds(pl.multiple_of(h * rows, rows), rows)

    def head_cols(who):
        return pl.ds(pl.multiple_of(who * hcols, hcols), hcols)

    def cols(c):
        return pl.ds(c * size if isinstance(c, int) else pl.multiple_of(c * size, size), size)

    def head_at(j):
        return pl.ds(j * HD if isinstance(j, int) else pl.multiple_of(j * HD, HD), HD)

    def own_copy(a):
        return pltpu.make_async_copy(
            fresh[a].at[0, :, head_cols(h)], fx.at[a, my_rows, :], x_in.at[x_sem[a]]
        )

    def remote(src, dst, send, recv, **to):
        return pltpu.make_async_remote_copy(
            src_ref=src, dst_ref=dst, send_sem=send, recv_sem=recv,
            device_id=to, device_id_type=MESH,
        )

    def wait_bytes(ref, sem):
        pltpu.make_async_copy(ref, ref, sem).wait()

    def load_text():
        pltpu.make_async_copy(mask, mk, t_in.at[0]).start()
        pltpu.make_async_copy(tk.at[0], tx.at[0], t_in.at[1]).start()
        pltpu.make_async_copy(tv.at[0], tx.at[1], t_in.at[1]).start()

    barrier = pltpu.get_barrier_semaphore()
    for k in range(1, n_head):
        pl.semaphore_signal(
            barrier, inc=1, device_id={"head": lax.rem(h + k, n_head)}, device_id_type=MESH
        )

    @pl.when(is_end)
    def _():
        pl.semaphore_signal(barrier, inc=1, device_id={"patch": inner}, device_id_type=MESH)

    @pl.when(jnp.logical_not(is_end))
    def _():
        pl.semaphore_signal(barrier, inc=1, device_id={"patch": across}, device_id_type=MESH)
        pl.semaphore_signal(barrier, inc=1, device_id={"patch": outer}, device_id_type=MESH)
        for i, ref in enumerate((sk, sv)):
            pltpu.make_async_copy(ref.at[0], kv.at[OWN, i], own_in.at[0]).start()

    for a in range(4):
        own_copy(a).start()
    load_text()
    pl.semaphore_wait(barrier, n_head - 1 + jnp.where(is_end, 1, 2))

    def send_x(a):
        for k in range(1, n_head):
            peer = lax.rem(h + k, n_head)
            remote(
                fresh[a].at[0, :, head_cols(peer)], fx.at[a, my_rows, :],
                sent.at[0], x_in.at[x_sem[a]], head=peer,
            ).start()

    def scores_of(q, keys):
        return dot_nt(q, keys) * scale

    def mix_of(weights, values):
        wide = jnp.concatenate([values, jnp.ones_like(values)], axis=1)
        mixed = jnp.dot(
            weights.astype(jnp.bfloat16), wide, preferred_element_type=jnp.float32
        )
        return mixed[:, :HD], mixed[:, HD:]

    def own_head(at):
        keys, values = (
            jnp.concatenate([fx[FK + i, :, at]] + [kv[s, i, :, at] for s in (END, ACROSS, FAR)])
            for i in range(2)
        )
        scores = scores_of(fx[FQ, :, at], keys)
        mix, total = mix_of(jnp.exp(scores - jnp.max(scores, axis=-1, keepdims=True)), values)
        return (mix / total).astype(jnp.bfloat16)

    def end_head(at, lse):
        keys, values = (
            jnp.concatenate([kv[s, i, :, at] for s in (END, ACROSS, FAR, OWN)]) for i in range(2)
        )
        scores = scores_of(dq[:, at], keys)
        padding = lax.broadcasted_iota(jnp.int32, scores.shape, 1) < prows
        scores = jnp.where(padding, -jnp.inf, scores)
        top = jnp.max(scores, axis=-1, keepdims=True)
        mix, total = mix_of(jnp.exp(scores - top), values)
        most = jnp.maximum(top, lse)
        mine = jnp.exp(top - most)
        theirs = jnp.exp(lse - most)
        mix = mix * mine + part[:, at].astype(jnp.float32) * theirs
        return (mix / (total * mine + theirs)).astype(jnp.bfloat16)

    def attend(c, both):
        results = []
        for i in range(cheads):
            j = c * cheads + i
            at = head_at(j)
            if both:
                results.append((oute, at, end_head(at, spread[j])))
            results.append((outs, at, own_head(at)))
        for ref, at, value in results:
            ref[:, at] = value

    def cross_heads(first, last):
        usable = mk[...] > 0

        def one(j):
            at = head_at(j)
            scores = jnp.where(usable, scores_of(fx[CQ, :, at], tx[0, :, at]), -jnp.inf)
            weights = jnp.exp(scores - jnp.max(scores, axis=-1, keepdims=True))
            total = jnp.sum(weights, axis=-1, keepdims=True)
            mix = jnp.dot(
                weights.astype(jnp.bfloat16), tx[1, :, at], preferred_element_type=jnp.float32
            )
            return at, (mix / total).astype(jnp.bfloat16)

        def step(s, carry):
            done = [one(first + s * CROSS + i) for i in range(CROSS)]
            for at, value in done:
                outc[:, at] = value
            return carry

        lax.fori_loop(0, (last - first) // CROSS, step, 0)
        for j in range(last - (last - first) % CROSS, last):
            at, value = one(j)
            outc[:, at] = value

    def out_at(dst, at):
        return dst.at[0, :, pl.ds(pl.multiple_of(h * hcols + at.start, HD), at.size)]

    def rows_of(src, who, at):
        return src.at[pl.ds(pl.multiple_of(who * rows, rows), rows), at]

    def send_out(src, dst, at, send, recv):
        for k in range(1, n_head):
            peer = lax.rem(h + k, n_head)
            remote(rows_of(src, peer, at), out_at(dst, at), send, recv, head=peer).start()
        pltpu.make_async_copy(rows_of(src, h, at), out_at(dst, at), recv).start()

    def wait_peers(src, at, send):
        if n_head > 1:
            wait_bytes(src.at[pl.ds(0, rows * (n_head - 1)), at], send)

    def send_cross():
        send_out(outc, co, every, sent.at[1], out_in.at[1])

    def wait_text():
        wait_bytes(mk, t_in.at[0])
        wait_bytes(tx, t_in.at[1])

    def end_program():
        def send_kv(c):
            for i, ref in enumerate((sk, sv)):
                remote(
                    ref.at[0, :, cols(c)], kv.at[END, i, :, cols(c)],
                    sent.at[2], end_in.at[c], patch=inner,
                ).start()

        lead = (nch + 1) // 2
        send_x(FQ)
        send_kv(0)
        send_x(FK)
        send_x(FV)
        send_x(CQ)
        for c in range(1, lead):
            send_kv(c)
        wait_bytes(fx.at[FQ], x_in.at[1])
        remote(
            fx.at[FQ, :, late], dq.at[:, late], sent.at[3], q_in.at[0], patch=inner
        ).start()
        for c in range(lead, nch):
            send_kv(c)
        wait_bytes(fx.at[pl.ds(FK, 2)], x_in.at[2])
        lanes = lax.broadcasted_iota(jnp.int32, (prows, HD), 1)
        lse = jnp.zeros((prows, HD), jnp.float32)
        for j in range(direct * cheads, heads):
            at = slice(j * HD, (j + 1) * HD)
            scores = scores_of(fx[FQ, :, at], fx[FK, :, at])
            top = jnp.max(scores, axis=-1, keepdims=True)
            mix, total = mix_of(jnp.exp(scores - top), fx[FV, :, at])
            outs[:, at] = (mix / total).astype(jnp.bfloat16)
            lse = jnp.where(lanes == j, top + jnp.log(total), lse)
        stat[1] = lse
        remote(
            outs.at[:, late], part.at[:, late], sent.at[4], part_in.at[0], patch=inner
        ).start()
        remote(stat.at[1], stat.at[0], sent.at[5], part_in.at[1], patch=inner).start()
        wait_text()
        wait_bytes(fx.at[CQ], x_in.at[0])
        cross_heads(0, heads)
        send_cross()

        def direct_chunk(c, carry):
            wait_bytes(kv.at[pl.ds(END, 3), :, :, cols(c)], far_in.at[c])
            attend(c, False)
            send_out(outs, so, cols(c), sent.at[6], out_in.at[0])
            return carry

        if direct:
            lax.fori_loop(0, direct, direct_chunk, 0)
        wait_bytes(kv.at[END], sent.at[2])
        wait_bytes(dq.at[:, late], sent.at[3])
        wait_bytes(part.at[:, late], sent.at[4])
        wait_bytes(stat.at[0], sent.at[5])
        if direct:
            wait_peers(outs, early, sent.at[6])

    def middle_program():
        def send_own(at, recv):
            for i, ref in enumerate((sk, sv)):
                remote(
                    ref.at[0, :, at], kv.at[ACROSS, i, :, at], sent.at[2], recv, patch=across
                ).start()

        def pass_out(src, slot, c):
            remote(
                src, kv.at[slot, :, :, cols(c)], sent.at[6], far_in.at[c], patch=outer
            ).start()

        def pass_across(c):
            src = kv.at[END, :, :, cols(c)]
            wait_bytes(src, end_in.at[c])
            remote(
                src, kv.at[FAR, :, :, cols(c)], sent.at[3], far_in.at[c], patch=across
            ).start()

        if direct:
            send_own(early, across_in.at[0])
        send_own(late, across_in.at[1])
        for a in (CQ, FQ, FK, FV):
            send_x(a)
        wait_bytes(kv.at[OWN], own_in.at[0])
        for c in range(direct):
            pass_out(kv.at[OWN, :, :, cols(c)], END, c)
        pass_across(0)
        wait_text()
        wait_bytes(fx.at[CQ], x_in.at[0])
        half = heads // 2
        cross_heads(0, half)
        if direct:
            wait_bytes(kv.at[ACROSS, :, :, early], across_in.at[0])
        for c in range(direct):
            pass_out(kv.at[ACROSS, :, :, cols(c)], ACROSS, c)
        if nch > 1:
            pass_across(1)
        cross_heads(half, heads)
        send_cross()
        for c in range(2, nch):
            pass_across(c)
        wait_bytes(fx.at[FQ], x_in.at[1])
        wait_bytes(fx.at[pl.ds(FK, 2)], x_in.at[2])
        wait_bytes(kv.at[ACROSS, :, :, late], across_in.at[1])
        def own_chunk(c, carry):
            far = kv.at[FAR, :, :, cols(c)]
            wait_bytes(far, far_in.at[c])
            pass_out(far, FAR, c)
            attend(c, False)
            send_out(outs, so, cols(c), sent.at[5], out_in.at[0])
            return carry

        def both_chunk(c, carry):
            wait_bytes(kv.at[FAR, :, :, cols(c)], far_in.at[c])
            attend(c, True)
            for k in range(n_head - 1, -1, -1):
                to = lax.rem(h + k, n_head)
                remote(
                    rows_of(oute, to, cols(c)), out_at(so, cols(c)),
                    sent.at[4], out_in.at[0], patch=outer, head=to,
                ).start()
            send_out(outs, so, cols(c), sent.at[5], out_in.at[0])
            return carry

        if direct:
            lax.fori_loop(0, direct, own_chunk, 0)
        wait_bytes(stat.at[0], part_in.at[1])
        for j in range(direct * cheads, heads):
            spread[j] = jnp.broadcast_to(stat[0, :, j : j + 1], (prows, HD))
        wait_bytes(dq.at[:, late], q_in.at[0])
        wait_bytes(part.at[:, late], part_in.at[0])
        lax.fori_loop(direct, nch, both_chunk, 0)
        wait_bytes(kv.at[ACROSS], sent.at[2])
        wait_bytes(kv.at[FAR], sent.at[3])
        wait_bytes(oute.at[:, late], sent.at[4])
        wait_peers(outs, every, sent.at[5])
        if direct:
            wait_bytes(kv.at[pl.ds(END, 3), :, :, early], sent.at[6])

    pl.when(is_end)(end_program)
    pl.when(jnp.logical_not(is_end))(middle_program)
    if n_head > 1:
        wait_bytes(fx.at[:, pl.ds(0, rows * (n_head - 1)), :], sent.at[0])
    wait_peers(outc, every, sent.at[1])
    wait_bytes(co, out_in.at[1])
    wait_bytes(so, out_in.at[0])


def quad_attention(n_head, *args):
    fq, fk, fv, sk, sv, cq, tk, tv, mask = args
    prows = fq.shape[1] * n_head
    hcols = sk.shape[2]
    heads = hcols // HD
    nch = heads // chunk_heads(heads)
    direct = min(DIRECT, nch - 1)
    txt = tk.shape[1]
    dma = pltpu.SemaphoreType.DMA
    bf16 = jnp.bfloat16
    patch = pltpu.VMEM((prows, hcols), bf16)
    return pl.pallas_call(
        functools.partial(quad_kernel, n_head, direct),
        out_shape=(pltpu.VMEM(fq.shape, bf16), pltpu.VMEM(cq.shape, bf16)),
        in_specs=[pl.BlockSpec(memory_space=pl.ANY)] * 9,
        out_specs=(pl.BlockSpec(memory_space=pltpu.VMEM),) * 2,
        scratch_shapes=[
            pltpu.VMEM((4, prows, hcols), bf16),
            pltpu.VMEM((4, 2, prows, hcols), bf16),
            pltpu.VMEM((2, txt, hcols), bf16),
            pltpu.VMEM((1, txt), jnp.int32),
            patch,
            patch,
            pltpu.VMEM((2, prows, HD), jnp.float32),
            pltpu.VMEM((heads, prows, HD), jnp.float32),
            patch,
            patch,
            patch,
            dma((3,)),
            dma((2,)),
            dma((1,)),
            dma((nch,)),
            dma((nch,)),
            dma((2,)),
            dma((1,)),
            dma((2,)),
            dma((2,)),
            dma((7,)),
        ],
        compiler_params=pltpu.CompilerParams(collective_id=0, has_side_effects=True),
        name="displaced_attention",
    )(*args)


def store_kernel(a, b, so, co, sem):
    copies = [
        pltpu.make_async_copy(a, so, sem.at[0]),
        pltpu.make_async_copy(b, co, sem.at[1]),
    ]
    for cp in copies:
        cp.start()
    for cp in copies:
        cp.wait()


def store(a, b):
    return pl.pallas_call(
        store_kernel,
        out_shape=(
            jax.ShapeDtypeStruct(a.shape, a.dtype),
            jax.ShapeDtypeStruct(b.shape, b.dtype),
        ),
        in_specs=[pl.BlockSpec(memory_space=pltpu.VMEM)] * 2,
        out_specs=(pl.BlockSpec(memory_space=pltpu.HBM),) * 2,
        scratch_shapes=[pltpu.SemaphoreType.DMA((2,))],
        compiler_params=pltpu.CompilerParams(vmem_limit_bytes=1024 * 1024),
        name="store_outputs",
    )(a, b)


def per_device(n_patch, n_head, *args):
    if n_patch == 4:
        return store(*quad_attention(n_head, *args))
    return store(*line_attention(n_patch, n_head, *args))


def solution(mesh):
    return jax.shard_map(
        functools.partial(per_device, mesh.shape["patch"], mesh.shape["head"]),
        mesh=mesh,
        in_specs=(
            P(("group", "cfg"), ("patch", "head"), None),
            P(("group", "cfg"), ("patch", "head"), None),
            P(("group", "cfg"), ("patch", "head"), None),
            P(("group", "cfg"), "patch", "head"),
            P(("group", "cfg"), "patch", "head"),
            P(("group", "cfg"), ("patch", "head"), None),
            P(("group", "cfg"), None, "head"),
            P(("group", "cfg"), None, "head"),
            P(("group", "cfg"), None),
        ),
        out_specs=(
            P(("group", "cfg"), ("patch", "head"), None),
            P(("group", "cfg"), ("patch", "head"), None),
        ),
        check_vma=False,
    )
```

```python
import functools
import math

import jax
import jax.numpy as jnp
from jax import lax
from jax.experimental import pallas as pl
from jax.experimental.pallas import tpu as pltpu
from jax.sharding import PartitionSpec as P

HD = 128
MESH = pl.DeviceIdType.MESH


def dot_nt(a, b):
    return lax.dot_general(a, b, (((1,), (1,)), ((), ())), preferred_element_type=jnp.float32)


def line_kernel(
    n_patch, n_head, nch,
    fq, fk, fv, sk, sv, cq, tk, tv, mask,
    so, co,
    fx, kv, txk, txv, mk, outs, outc,
    x_send, x_recv, x_loc, t_loc, kv_loc, own_send, fwd_send, kv_recv,
    o_send, o_recv, o_loc, c_send, c_recv, c_loc,
):
    p = lax.axis_index("patch")
    h = lax.axis_index("head")
    rows = fq.shape[1]
    prows = rows * n_head
    hcols = sk.shape[2]
    ccols = hcols // nch
    heads = hcols // HD
    cheads = heads // nch
    scale = 1.0 / math.sqrt(HD)
    fresh = (cq, fq, fk, fv)
    my_rows = pl.ds(pl.multiple_of(h * rows, rows), rows)

    for c in range(nch):
        for i, ref in enumerate((sk, sv)):
            pltpu.make_async_copy(
                ref.at[0, :, pl.ds(c * ccols, ccols)], kv.at[p, c, i], kv_loc.at[c, i]
            ).start()
    text_copies = [
        pltpu.make_async_copy(mask, mk, t_loc.at[0]),
        pltpu.make_async_copy(tk.at[0], txk, t_loc.at[1]),
        pltpu.make_async_copy(tv.at[0], txv, t_loc.at[2]),
    ]
    own_copies = [
        pltpu.make_async_copy(
            ref.at[0, :, pl.ds(pl.multiple_of(h * hcols, hcols), hcols)],
            fx.at[a, my_rows, :],
            x_loc.at[a],
        )
        for a, ref in enumerate(fresh)
    ]
    for cp in own_copies + text_copies:
        cp.start()

    barrier = pltpu.get_barrier_semaphore()
    has_right = p < n_patch - 1
    has_left = p > 0

    @pl.when(has_right)
    def _():
        pl.semaphore_signal(barrier, inc=1, device_id={"patch": p + 1}, device_id_type=MESH)

    @pl.when(has_left)
    def _():
        pl.semaphore_signal(barrier, inc=1, device_id={"patch": p - 1}, device_id_type=MESH)

    for k in range(1, n_head):
        pl.semaphore_signal(
            barrier, inc=1, device_id={"head": lax.rem(h + k, n_head)}, device_id_type=MESH
        )
    pl.semaphore_wait(
        barrier, n_head - 1 + has_right.astype(jnp.int32) + has_left.astype(jnp.int32)
    )

    def x_copy(a, k):
        peer = lax.rem(h + k, n_head)
        return pltpu.make_async_remote_copy(
            src_ref=fresh[a].at[0, :, pl.ds(pl.multiple_of(peer * hcols, hcols), hcols)],
            dst_ref=fx.at[a, my_rows, :],
            send_sem=x_send.at[a, k - 1],
            recv_sem=x_recv.at[a, k - 1],
            device_id={"head": peer},
            device_id_type=MESH,
        )

    def kv_copy(src, c, target, sem):
        return pltpu.make_async_remote_copy(
            src_ref=kv.at[src, c],
            dst_ref=kv.at[src, c],
            send_sem=sem,
            recv_sem=kv_recv.at[src, c],
            device_id={"patch": target},
            device_id_type=MESH,
        )

    def start_x():
        for a in (1, 0, 2, 3):
            for k in range(1, n_head):
                x_copy(a, k).start()

    def wait_own_kv(c):
        for i, ref in enumerate((sk, sv)):
            pltpu.make_async_copy(
                ref.at[0, :, pl.ds(c * ccols, ccols)], kv.at[p, c, i], kv_loc.at[c, i]
            ).wait()

    def wait_x(a):
        own_copies[a].wait()
        for k in range(1, n_head):
            x_copy(a, k).wait_recv()

    def out_copy(src, dst, c, k, send, recv):
        peer = lax.rem(h + k, n_head)
        return pltpu.make_async_remote_copy(
            src_ref=src.at[c, pl.ds(pl.multiple_of(peer * rows, rows), rows), :],
            dst_ref=dst.at[0, :, pl.ds(pl.multiple_of(h * hcols + c * ccols, HD), ccols)],
            send_sem=send.at[c, k - 1],
            recv_sem=recv.at[c, k - 1],
            device_id={"head": peer},
            device_id_type=MESH,
        )

    def local_out(src, dst, c, sem):
        return pltpu.make_async_copy(
            src.at[c, my_rows, :],
            dst.at[0, :, pl.ds(pl.multiple_of(h * hcols + c * ccols, HD), ccols)],
            sem.at[c],
        )

    def send_out(src, dst, c, send, recv, loc):
        for k in range(1, n_head):
            out_copy(src, dst, c, k, send, recv).start()
        local_out(src, dst, c, loc).start()

    def cross_chunk(c):
        usable = mk[...] > 0
        for i in range(cheads):
            cols = pl.ds((c * cheads + i) * HD, HD)
            scores = dot_nt(fx[0, :, cols], txk[:, cols]) * scale
            scores = jnp.where(usable, scores, -jnp.inf)
            top = jnp.max(scores, axis=-1, keepdims=True)
            weights = jnp.exp(scores - top)
            total = jnp.sum(weights, axis=-1, keepdims=True)
            mix = jnp.dot(
                weights.astype(jnp.bfloat16), txv[:, cols], preferred_element_type=jnp.float32
            )
            outc[c, :, i * HD : (i + 1) * HD] = (mix / total).astype(jnp.bfloat16)

    def query(j):
        return fx[1, :, pl.ds(j * HD, HD)]

    def weigh(q, keys, values, top=None):
        scores = dot_nt(q, keys) * scale
        new_top = jnp.max(scores, axis=-1, keepdims=True)
        if top is not None:
            new_top = jnp.maximum(top, new_top)
        weights = jnp.exp(scores - new_top).astype(jnp.bfloat16)
        wide = jnp.concatenate([values, jnp.ones_like(values)], axis=1)
        mixed = jnp.dot(weights, wide, preferred_element_type=jnp.float32)
        return new_top, mixed[:, HD:], mixed[:, :HD]

    def absorb_rows(state, q, keys, values):
        top, total, mix = state
        new_top, more_total, more_mix = weigh(q, keys, values, top)
        factor = jnp.exp(top - new_top)
        return new_top, total * factor + more_total, mix * factor + more_mix

    def kv_rows(i, j, *sources):
        c, k = divmod(j, cheads)
        parts = [kv[src, c, i, :, pl.ds(k * HD, HD)] for src in sources]
        return parts[0] if len(parts) == 1 else jnp.concatenate(parts, axis=0)

    def fresh_rows(i, j):
        return fx[2 + i, :, pl.ds(j * HD, HD)]

    def first(j):
        return weigh(query(j), fresh_rows(0, j), fresh_rows(1, j))

    def absorb(state, src, j):
        return absorb_rows(state, query(j), kv_rows(0, j, src), kv_rows(1, j, src))

    def line_program():
        start_x()
        for c in range(nch):
            wait_own_kv(c)

            @pl.when(has_right)
            def _():
                kv_copy(p, c, p + 1, own_send.at[0, c]).start()

            @pl.when(has_left)
            def _():
                kv_copy(p, c, p - 1, own_send.at[1, c]).start()

        shorter = jnp.minimum(p, n_patch - 1 - p)

        def slot_source(s):
            near = s // 2 + 1
            near_src = jnp.where(s % 2 == 0, p - near, p + near)
            far = s - shorter + 1
            far_src = jnp.where(p > shorter, p - far, p + far)
            return jnp.where(s < 2 * shorter, near_src, far_src)

        def forward_target(src):
            target = jnp.where(src < p, p + 1, p - 1)
            return target, (target >= 0) & (target < n_patch)

        def forward(s, c):
            src = slot_source(s)
            kv_copy(src, c, p, fwd_send.at[s, c]).wait_recv()
            target, valid = forward_target(src)

            @pl.when(valid)
            def _():
                kv_copy(src, c, target, fwd_send.at[s, c]).start()

        half = (nch + 1) // 2
        for cp in text_copies:
            cp.wait()
        wait_x(0)
        for c in range(half):
            cross_chunk(c)
        for c in range(half):
            forward(0, c)
        for c in range(half, nch):
            cross_chunk(c)
        for c in range(nch):
            send_out(outc, co, c, c_send, c_recv, c_loc)
        for c in range(half, nch):
            forward(0, c)
        for a in range(1, 4):
            wait_x(a)
        states = [first(j) for j in range(heads)]
        src = slot_source(0)
        states = [absorb(states[j], src, j) for j in range(heads)]

        def slot(s, states):
            src = slot_source(s)
            out = []
            for c in range(nch):
                forward(s, c)
                for j in range(c * cheads, (c + 1) * cheads):
                    out.append(absorb(states[j], src, j))
            return out

        if n_patch <= 8:
            for s in range(1, n_patch - 2):
                states = slot(s, states)
        else:
            states = lax.fori_loop(1, n_patch - 2, slot, states)
        last = n_patch - 2
        src = slot_source(last)
        for c in range(nch):
            if last > 0:
                forward(last, c)
            for i in range(cheads):
                j = c * cheads + i
                _, total, mix = absorb(states[j], src, j) if last > 0 else states[j]
                outs[c, :, i * HD : (i + 1) * HD] = (mix / total).astype(jnp.bfloat16)
            if c > 0:
                send_out(outs, so, c - 1, o_send, o_recv, o_loc)
        send_out(outs, so, nch - 1, o_send, o_recv, o_loc)

        for c in range(nch):

            @pl.when(has_right)
            def _():
                kv_copy(p, c, p + 1, own_send.at[0, c]).wait_send()

            @pl.when(has_left)
            def _():
                kv_copy(p, c, p - 1, own_send.at[1, c]).wait_send()

        def drain(s, carry):
            for c in range(nch):
                target, valid = forward_target(slot_source(s))

                @pl.when(valid)
                def _():
                    kv_copy(slot_source(s), c, target, fwd_send.at[s, c]).wait_send()

            return carry

        if n_patch <= 8:
            for s in range(n_patch - 1):
                drain(s, 0)
        else:
            lax.fori_loop(0, n_patch - 1, drain, 0)

    line_program()

    for a in range(4):
        for k in range(1, n_head):
            x_copy(a, k).wait_send()
    for src_ref, dst, send, recv, loc in (
        (outc, co, c_send, c_recv, c_loc),
        (outs, so, o_send, o_recv, o_loc),
    ):
        for c in range(nch):
            for k in range(1, n_head):
                cp = out_copy(src_ref, dst, c, k, send, recv)
                cp.wait_send()
                cp.wait_recv()
            local_out(src_ref, dst, c, loc).wait()


def line_attention(n_patch, n_head, *args):
    fq, fk, fv, sk, sv, cq, tk, tv, mask = args
    rows = fq.shape[1]
    prows = rows * n_head
    hcols = sk.shape[2]
    heads = hcols // HD
    nch = 2 if heads % 2 == 0 else 1
    ccols = hcols // nch
    txt = tk.shape[1]
    peers = max(n_head - 1, 1)
    any_spec = pl.BlockSpec(memory_space=pl.ANY)
    dma = pltpu.SemaphoreType.DMA
    bf16 = jnp.bfloat16
    mixed = pl.pallas_call(
        functools.partial(line_kernel, n_patch, n_head, nch),
        out_shape=(
            pltpu.VMEM(fq.shape, bf16),
            pltpu.VMEM(cq.shape, bf16),
        ),
        in_specs=[any_spec] * 9,
        out_specs=(pl.BlockSpec(memory_space=pltpu.VMEM),) * 2,
        scratch_shapes=[
            pltpu.VMEM((4, prows, hcols), bf16),
            pltpu.VMEM((n_patch, nch, 2, prows, ccols), bf16),
            pltpu.VMEM((txt, hcols), bf16),
            pltpu.VMEM((txt, hcols), bf16),
            pltpu.VMEM((1, txt), jnp.int32),
            pltpu.VMEM((nch, prows, ccols), bf16),
            pltpu.VMEM((nch, prows, ccols), bf16),
            dma((4, peers)),
            dma((4, peers)),
            dma((4,)),
            dma((3,)),
            dma((nch, 2)),
            dma((2, nch)),
            dma((n_patch, nch)),
            dma((n_patch, nch)),
            dma((nch, peers)),
            dma((nch, peers)),
            dma((nch,)),
            dma((nch, peers)),
            dma((nch, peers)),
            dma((nch,)),
        ],
        compiler_params=pltpu.CompilerParams(collective_id=0, has_side_effects=True),
        name="displaced_attention",
    )(*args)
    return mixed


END, ACROSS, FAR, OWN = range(4)
CQ, FQ, FK, FV = range(4)
DIRECT = 2
CROSS = 2


def chunk_heads(heads):
    return max(n for n in range(1, max(1, heads // 5) + 1) if heads % n == 0)


def quad_kernel(
    n_head, direct,
    fq, fk, fv, sk, sv, cq, tk, tv, mask,
    so, co,
    fx, kv, tx, mk, dq, part, stat, spread, outs, oute, outc,
    x_in, t_in, own_in, end_in, far_in, across_in, q_in, part_in, out_in, sent, ready,
):
    p = lax.axis_index("patch")
    h = lax.axis_index("head")
    rows = fq.shape[1]
    prows = rows * n_head
    hcols = sk.shape[2]
    heads = hcols // HD
    cheads = chunk_heads(heads)
    nch = heads // cheads
    size = cheads * HD
    early = pl.ds(0, direct * size)
    late = pl.ds(direct * size, hcols - direct * size)
    every = pl.ds(0, hcols)
    scale = 1.0 / math.sqrt(HD)
    fresh = (cq, fq, fk, fv)
    x_sem = (0, 1, 2, 2)
    across = 3 - p
    is_end = (p == 0) | (p == 3)
    inner = jnp.where(p < 2, 1, 2)
    outer = jnp.where(p < 2, 0, 3)
    my_rows = pl.ds(pl.multiple_of(h * rows, rows), rows)

    def head_cols(who):
        return pl.ds(pl.multiple_of(who * hcols, hcols), hcols)

    def cols(c):
        return pl.ds(c * size if isinstance(c, int) else pl.multiple_of(c * size, size), size)

    def head_at(j):
        return pl.ds(j * HD if isinstance(j, int) else pl.multiple_of(j * HD, HD), HD)

    def own_copy(a):
        return pltpu.make_async_copy(
            fresh[a].at[0, :, head_cols(h)], fx.at[a, my_rows, :], x_in.at[x_sem[a]]
        )

    def remote(src, dst, send, recv, **to):
        return pltpu.make_async_remote_copy(
            src_ref=src, dst_ref=dst, send_sem=send, recv_sem=recv,
            device_id=to, device_id_type=MESH,
        )

    def wait_bytes(ref, sem):
        pltpu.make_async_copy(ref, ref, sem).wait()

    def load_text():
        pltpu.make_async_copy(mask, mk, t_in.at[0]).start()
        pltpu.make_async_copy(tk.at[0], tx.at[0], t_in.at[1]).start()
        pltpu.make_async_copy(tv.at[0], tx.at[1], t_in.at[1]).start()

    barrier = pltpu.get_barrier_semaphore()

    def greet(**to):
        pl.semaphore_signal(barrier, inc=1, device_id=to, device_id_type=MESH)

    @pl.when(is_end)
    def _():
        for k in range(1, n_head):
            greet(head=lax.rem(h + k, n_head))

    @pl.when(jnp.logical_not(is_end))
    def _():
        greet(patch=across)
        for k in range(1, n_head):
            pl.when(h + k < n_head)(functools.partial(greet, head=h + k))
        greet(patch=outer)
        for i, ref in enumerate((sk, sv)):
            pltpu.make_async_copy(ref.at[0], kv.at[OWN, i], own_in.at[0]).start()

    for a in range(4):
        own_copy(a).start()
    load_text()
    pl.semaphore_wait(barrier, 1 + jnp.where(is_end, n_head - 1, h))

    def send_x(a):
        for k in range(1, n_head):
            peer = lax.rem(h + k, n_head)
            remote(
                fresh[a].at[0, :, head_cols(peer)], fx.at[a, my_rows, :],
                sent.at[0], x_in.at[x_sem[a]], head=peer,
            ).start()

    def scores_of(q, keys):
        return dot_nt(q, keys) * scale

    def mix_of(weights, values):
        wide = jnp.concatenate([values, jnp.ones_like(values)], axis=1)
        mixed = jnp.dot(
            weights.astype(jnp.bfloat16), wide, preferred_element_type=jnp.float32
        )
        return mixed[:, :HD], mixed[:, HD:]

    def own_head(at):
        keys, values = (
            jnp.concatenate([fx[FK + i, :, at]] + [kv[s, i, :, at] for s in (END, ACROSS, FAR)])
            for i in range(2)
        )
        scores = scores_of(fx[FQ, :, at], keys)
        mix, total = mix_of(jnp.exp(scores - jnp.max(scores, axis=-1, keepdims=True)), values)
        return (mix / total).astype(jnp.bfloat16)

    def end_head(at, lse):
        keys, values = (
            jnp.concatenate([kv[s, i, :, at] for s in (END, ACROSS, FAR, OWN)]) for i in range(2)
        )
        scores = scores_of(dq[:, at], keys)
        padding = lax.broadcasted_iota(jnp.int32, scores.shape, 1) < prows
        scores = jnp.where(padding, -jnp.inf, scores)
        top = jnp.max(scores, axis=-1, keepdims=True)
        mix, total = mix_of(jnp.exp(scores - top), values)
        most = jnp.maximum(top, lse)
        mine = jnp.exp(top - most)
        theirs = jnp.exp(lse - most)
        mix = mix * mine + part[:, at].astype(jnp.float32) * theirs
        return (mix / (total * mine + theirs)).astype(jnp.bfloat16)

    def attend(c, both):
        results = []
        for i in range(cheads):
            j = c * cheads + i
            at = head_at(j)
            if both:
                results.append((oute, at, end_head(at, spread[j])))
            results.append((outs, at, own_head(at)))
        for ref, at, value in results:
            ref[:, at] = value

    def cross_heads(first, last):
        usable = mk[...] > 0

        def one(j):
            at = head_at(j)
            scores = jnp.where(usable, scores_of(fx[CQ, :, at], tx[0, :, at]), -jnp.inf)
            weights = jnp.exp(scores - jnp.max(scores, axis=-1, keepdims=True))
            total = jnp.sum(weights, axis=-1, keepdims=True)
            mix = jnp.dot(
                weights.astype(jnp.bfloat16), tx[1, :, at], preferred_element_type=jnp.float32
            )
            return at, (mix / total).astype(jnp.bfloat16)

        def step(s, carry):
            done = [one(first + s * CROSS + i) for i in range(CROSS)]
            for at, value in done:
                outc[:, at] = value
            return carry

        lax.fori_loop(0, (last - first) // CROSS, step, 0)
        for j in range(last - (last - first) % CROSS, last):
            at, value = one(j)
            outc[:, at] = value

    def out_at(dst, at):
        return dst.at[0, :, pl.ds(pl.multiple_of(h * hcols + at.start, HD), at.size)]

    def rows_of(src, who, at):
        return src.at[pl.ds(pl.multiple_of(who * rows, rows), rows), at]

    def send_out(src, dst, at, send, recv):
        for k in range(1, n_head):
            peer = lax.rem(h + k, n_head)
            remote(rows_of(src, peer, at), out_at(dst, at), send, recv, head=peer).start()
        pltpu.make_async_copy(rows_of(src, h, at), out_at(dst, at), recv).start()

    def wait_peers(src, at, send):
        if n_head > 1:
            wait_bytes(src.at[pl.ds(0, rows * (n_head - 1)), at], send)

    def send_cross():
        send_out(outc, co, every, sent.at[1], out_in.at[1])

    def wait_text():
        wait_bytes(mk, t_in.at[0])
        wait_bytes(tx, t_in.at[1])

    def end_program():
        def send_kv(c):
            for i, ref in enumerate((sk, sv)):
                remote(
                    ref.at[0, :, cols(c)], kv.at[END, i, :, cols(c)],
                    sent.at[2], end_in.at[c], patch=inner,
                ).start()

        lead = (nch + 1) // 2
        send_x(FQ)
        send_kv(0)
        send_x(FK)
        send_x(FV)
        send_x(CQ)
        for c in range(1, lead):
            send_kv(c)

        def send_rest():
            for c in range(lead, nch):
                send_kv(c)

        pl.when(p != 0)(send_rest)
        wait_bytes(fx.at[FQ], x_in.at[1])
        remote(
            fx.at[FQ, :, late], dq.at[:, late], sent.at[3], q_in.at[0], patch=inner
        ).start()
        pl.when(p == 0)(send_rest)
        wait_bytes(fx.at[pl.ds(FK, 2)], x_in.at[2])
        lanes = lax.broadcasted_iota(jnp.int32, (prows, HD), 1)
        lse = jnp.zeros((prows, HD), jnp.float32)
        for j in range(direct * cheads, heads):
            at = slice(j * HD, (j + 1) * HD)
            scores = scores_of(fx[FQ, :, at], fx[FK, :, at])
            top = jnp.max(scores, axis=-1, keepdims=True)
            mix, total = mix_of(jnp.exp(scores - top), fx[FV, :, at])
            outs[:, at] = (mix / total).astype(jnp.bfloat16)
            lse = jnp.where(lanes == j, top + jnp.log(total), lse)
        stat[1] = lse
        remote(
            outs.at[:, late], part.at[:, late], sent.at[4], part_in.at[0], patch=inner
        ).start()
        remote(stat.at[1], stat.at[0], sent.at[5], part_in.at[1], patch=inner).start()
        wait_text()
        wait_bytes(fx.at[CQ], x_in.at[0])
        cross_heads(0, heads)
        send_cross()

        def direct_chunk(c, carry):
            wait_bytes(kv.at[pl.ds(END, 3), :, :, cols(c)], far_in.at[c])
            attend(c, False)
            send_out(outs, so, cols(c), sent.at[6], out_in.at[0])
            return carry

        if direct:
            lax.fori_loop(0, direct, direct_chunk, 0)
        wait_bytes(kv.at[END], sent.at[2])
        wait_bytes(dq.at[:, late], sent.at[3])
        wait_bytes(part.at[:, late], sent.at[4])
        wait_bytes(stat.at[0], sent.at[5])
        if direct:
            wait_peers(outs, early, sent.at[6])

    def middle_program():
        def send_own(at, recv):
            for i, ref in enumerate((sk, sv)):
                remote(
                    ref.at[0, :, at], kv.at[ACROSS, i, :, at], sent.at[2], recv, patch=across
                ).start()

        def pass_out(src, slot, c):
            remote(
                src, kv.at[slot, :, :, cols(c)], sent.at[6], far_in.at[c], patch=outer
            ).start()

        def pass_across(c):
            src = kv.at[END, :, :, cols(c)]
            wait_bytes(src, end_in.at[c])
            remote(
                src, kv.at[FAR, :, :, cols(c)], sent.at[3], far_in.at[c], patch=across
            ).start()

        if direct:
            send_own(early, across_in.at[0])
        send_own(late, across_in.at[1])
        for k in range(1, n_head):

            @pl.when(h - k >= 0)
            def _():
                pl.semaphore_signal(
                    ready, inc=1, device_id={"head": h - k}, device_id_type=MESH
                )

        @pl.when(h < n_head - 1)
        def _():
            pl.semaphore_wait(ready, n_head - 1 - h)

        for a in (CQ, FQ, FK, FV):
            send_x(a)
        wait_bytes(kv.at[OWN], own_in.at[0])
        pass_across(0)
        for c in range(direct):
            pass_out(kv.at[OWN, :, :, cols(c)], END, c)
        wait_text()
        wait_bytes(fx.at[CQ], x_in.at[0])
        half = heads // 2
        cross_heads(0, half)
        if direct:
            wait_bytes(kv.at[ACROSS, :, :, early], across_in.at[0])
        for c in range(direct):
            pass_out(kv.at[ACROSS, :, :, cols(c)], ACROSS, c)
        if nch > 1:
            pass_across(1)
        cross_heads(half, heads)
        send_cross()
        for c in range(2, nch):
            pass_across(c)
        wait_bytes(fx.at[FQ], x_in.at[1])
        wait_bytes(fx.at[pl.ds(FK, 2)], x_in.at[2])
        wait_bytes(kv.at[ACROSS, :, :, late], across_in.at[1])
        def own_chunk(c, carry):
            far = kv.at[FAR, :, :, cols(c)]
            wait_bytes(far, far_in.at[c])
            pass_out(far, FAR, c)
            attend(c, False)
            send_out(outs, so, cols(c), sent.at[5], out_in.at[0])
            return carry

        def both_chunk(c, carry):
            wait_bytes(kv.at[FAR, :, :, cols(c)], far_in.at[c])
            attend(c, True)
            for k in range(n_head - 1, -1, -1):
                to = lax.rem(h + k, n_head)
                remote(
                    rows_of(oute, to, cols(c)), out_at(so, cols(c)),
                    sent.at[4], out_in.at[0], patch=outer, head=to,
                ).start()
            send_out(outs, so, cols(c), sent.at[5], out_in.at[0])
            return carry

        if direct:
            lax.fori_loop(0, direct, own_chunk, 0)
        wait_bytes(stat.at[0], part_in.at[1])
        for j in range(direct * cheads, heads):
            spread[j] = jnp.broadcast_to(stat[0, :, j : j + 1], (prows, HD))
        wait_bytes(dq.at[:, late], q_in.at[0])
        wait_bytes(part.at[:, late], part_in.at[0])
        lax.fori_loop(direct, nch, both_chunk, 0)
        wait_bytes(kv.at[ACROSS], sent.at[2])
        wait_bytes(kv.at[FAR], sent.at[3])
        wait_bytes(oute.at[:, late], sent.at[4])
        wait_peers(outs, every, sent.at[5])
        if direct:
            wait_bytes(kv.at[pl.ds(END, 3), :, :, early], sent.at[6])

    pl.when(is_end)(end_program)
    pl.when(jnp.logical_not(is_end))(middle_program)
    if n_head > 1:
        wait_bytes(fx.at[:, pl.ds(0, rows * (n_head - 1)), :], sent.at[0])
    wait_peers(outc, every, sent.at[1])
    wait_bytes(co, out_in.at[1])
    wait_bytes(so, out_in.at[0])


def quad_attention(n_head, *args):
    fq, fk, fv, sk, sv, cq, tk, tv, mask = args
    prows = fq.shape[1] * n_head
    hcols = sk.shape[2]
    heads = hcols // HD
    nch = heads // chunk_heads(heads)
    direct = min(DIRECT, nch - 1)
    txt = tk.shape[1]
    dma = pltpu.SemaphoreType.DMA
    bf16 = jnp.bfloat16
    patch = pltpu.VMEM((prows, hcols), bf16)
    return pl.pallas_call(
        functools.partial(quad_kernel, n_head, direct),
        out_shape=(pltpu.VMEM(fq.shape, bf16), pltpu.VMEM(cq.shape, bf16)),
        in_specs=[pl.BlockSpec(memory_space=pl.ANY)] * 9,
        out_specs=(pl.BlockSpec(memory_space=pltpu.VMEM),) * 2,
        scratch_shapes=[
            pltpu.VMEM((4, prows, hcols), bf16),
            pltpu.VMEM((4, 2, prows, hcols), bf16),
            pltpu.VMEM((2, txt, hcols), bf16),
            pltpu.VMEM((1, txt), jnp.int32),
            patch,
            patch,
            pltpu.VMEM((2, prows, HD), jnp.float32),
            pltpu.VMEM((heads, prows, HD), jnp.float32),
            patch,
            patch,
            patch,
            dma((3,)),
            dma((2,)),
            dma((1,)),
            dma((nch,)),
            dma((nch,)),
            dma((2,)),
            dma((1,)),
            dma((2,)),
            dma((2,)),
            dma((7,)),
            pltpu.SemaphoreType.REGULAR,
        ],
        compiler_params=pltpu.CompilerParams(collective_id=0, has_side_effects=True),
        name="displaced_attention",
    )(*args)


def store_kernel(a, b, so, co, sem):
    copies = [
        pltpu.make_async_copy(a, so, sem.at[0]),
        pltpu.make_async_copy(b, co, sem.at[1]),
    ]
    for cp in copies:
        cp.start()
    for cp in copies:
        cp.wait()


def store(a, b):
    return pl.pallas_call(
        store_kernel,
        out_shape=(
            jax.ShapeDtypeStruct(a.shape, a.dtype),
            jax.ShapeDtypeStruct(b.shape, b.dtype),
        ),
        in_specs=[pl.BlockSpec(memory_space=pltpu.VMEM)] * 2,
        out_specs=(pl.BlockSpec(memory_space=pltpu.HBM),) * 2,
        scratch_shapes=[pltpu.SemaphoreType.DMA((2,))],
        compiler_params=pltpu.CompilerParams(vmem_limit_bytes=1024 * 1024),
        name="store_outputs",
    )(a, b)


def per_device(n_patch, n_head, *args):
    if n_patch == 4:
        return store(*quad_attention(n_head, *args))
    return store(*line_attention(n_patch, n_head, *args))


def solution(mesh):
    return jax.shard_map(
        functools.partial(per_device, mesh.shape["patch"], mesh.shape["head"]),
        mesh=mesh,
        in_specs=(
            P(("group", "cfg"), ("patch", "head"), None),
            P(("group", "cfg"), ("patch", "head"), None),
            P(("group", "cfg"), ("patch", "head"), None),
            P(("group", "cfg"), "patch", "head"),
            P(("group", "cfg"), "patch", "head"),
            P(("group", "cfg"), ("patch", "head"), None),
            P(("group", "cfg"), None, "head"),
            P(("group", "cfg"), None, "head"),
            P(("group", "cfg"), None),
        ),
        out_specs=(
            P(("group", "cfg"), ("patch", "head"), None),
            P(("group", "cfg"), ("patch", "head"), None),
        ),
        check_vma=False,
    )
```
